32 devices in a mesh: space: 16 (over z, y, core), chan: 2 (over x).
Axes of the slice: x: 2, y: 2, z: 4, core: 2. Of those that a mesh axis runs over, the one named last changes fastest.
Arguments:
- volume: float32 [32, 32, 128, 128], P('chan', 'space'), may hold values from -6 to 6
- filters: float32 [64, 32, 3, 3, 3], P(None, 'chan'), may hold values from -0.21875 to 0.21875
- cotangent: float32 [64, 16, 64, 64], P('chan', 'space'), may hold values from -6 to 6
Outputs:
- activated: float32 [64, 16, 64, 64], P('chan', 'space')
- volume_grad: float32 [32, 32, 128, 128], P('chan', 'space')
- filter_grad: float32 [64, 32, 3, 3, 3], P(None, 'chan')
The draws below stay inside these ranges and needn't reach their ends.
All inputs are finite; a program needn't handle non-finite values.
Results may differ from the reference program's by a relative error of at most 0.00014.
Values sent between devices are 32-bit elements; how exact they have to be, the bound alone decides.
No kernel may reach another device: no remote copies, remote signals or barrier semaphores. Data moves between devices by JAX's collectives and lax.ppermute only.
A program may use at most 192 MiB of HBM per device.

```python
import jax
import jax.numpy as jnp
from jax import lax

CIN = 32
COUT = 64
PLANE = 128
NZ = 32


def levels(own_key, extent, cuts, low, largest):
    gain = 1.0
    for dim, parts in cuts:
        heights = jax.random.uniform(jax.random.fold_in(jax.random.fold_in(own_key, 6), dim), (parts,), jnp.float32, low / len(cuts), largest / len(cuts))
        gain = gain * jnp.repeat(jnp.exp(heights), extent[dim] // parts).reshape((-1,) + (1,) * (len(extent) - 1 - dim))
    return gain


def gaussian(key, dims, spread, limit, split=(), held_as=jnp.bfloat16):
    entries = spread * jax.random.normal(key, dims, jnp.float32)
    if split:
        entries = entries * levels(key, dims, split, -0.22, 0.18)
    return jnp.clip(entries, -limit, limit).astype(held_as)


def setup_inputs(seed: int = 0) -> dict:
    key_list = jax.random.split(jax.random.key(seed), 4)
    volume = gaussian(key_list[0], (CIN, NZ, PLANE, PLANE), 1.0, 6.0, ((0, 2), (1, 16)), jnp.float32)
    filters = gaussian(key_list[1], (COUT, CIN, 3, 3, 3), (CIN * 27) ** -0.5, 0.21875, ((1, 2),), jnp.float32)
    cotangent = gaussian(key_list[2], (COUT, NZ // 2, PLANE // 2, PLANE // 2), 1.0, 6.0, ((0, 2), (1, 16)), jnp.float32)
    return {"volume": volume, "filters": filters, "cotangent": cotangent}


def convolve(volume, filters):
    result = lax.conv_general_dilated(volume[None], filters, (2, 2, 2), ((1, 1), (1, 1), (1, 1)), dimension_numbers=('NCDHW', 'OIDHW', 'NCDHW'), precision=lax.Precision.HIGHEST)
    return result[0]

def reference(volume, filters, cotangent):
    preact, pullback = jax.vjp(convolve, volume, filters)
    activated = jax.nn.softplus(preact)
    preact_grad = cotangent * jax.nn.sigmoid(preact)
    volume_grad, filter_grad = pullback(preact_grad)
    factor = float(NZ // 2 * (PLANE // 2) * (PLANE // 2)) ** (-0.5)
    return (activated, volume_grad, filter_grad * factor)
```

```python
import functools

import jax
import jax.numpy as jnp
from jax import lax
from jax.experimental import pallas as pl
from jax.experimental.pallas import tpu as pltpu
from jax.sharding import PartitionSpec as P

F32 = jnp.float32
BF16 = jnp.bfloat16
LANES = 128
STEP = 4
VMEM = pl.BlockSpec(memory_space=pltpu.VMEM)

PLACE = {0: (1, 1), 1: (0, 0), 2: (1, 0)}


def split(x):
    hi = x.astype(BF16)
    return hi, (x - hi.astype(F32)).astype(BF16)


def pairing(half, transposed):
    size = 4 * half
    cell = lax.broadcasted_iota(jnp.int32, (size, size), 0 if transposed else 1)
    source = lax.broadcasted_iota(jnp.int32, (size, size), 1 if transposed else 0)
    parity, rest = cell // (2 * half), cell % (2 * half)
    wanted = (rest // half) * (2 * half) + 2 * (rest % half) + parity
    return (source == wanted).astype(F32).astype(BF16)


def lane_of(shape):
    return lax.broadcasted_iota(jnp.int32, shape, 1)


def parity_split(load, planes, step, matrix, half):
    tiles = []
    for plane in range(planes):
        for parity in range(2):
            for j in range(STEP):
                row = 4 * (step * STEP + j) + parity
                tiles.append(jnp.concatenate([load(plane, row), load(plane, row + 2)], axis=1))
    chans = tiles[0].shape[0]
    hi, lo = split(jnp.concatenate(tiles, axis=0))
    moved = jnp.dot(jnp.concatenate([hi, lo], axis=0), matrix, preferred_element_type=F32).astype(BF16)
    parts = []
    for part in range(2):
        rows = []
        for group in range(planes * 2):
            for column in range(2):
                pieces = []
                for j in range(STEP):
                    start = ((part * planes * 2 + group) * STEP + j) * chans
                    pieces.append(moved[start : start + chans, column * LANES : (column + 1) * LANES])
                rows.append(jnp.concatenate(pieces, axis=1))
        parts.append(jnp.concatenate(rows, axis=0))
    return parts


def shift_add(y, outs, half, carry):
    lane = lane_of((outs, LANES))
    first_column = lane % half == 0
    first_row = lane < half

    def one_column(v):
        return jnp.where(first_column, 0.0, pltpu.roll(v, 1, 1))

    pieces = []
    for j in range(STEP):
        v = [y[s * outs : (s + 1) * outs, j * LANES : (j + 1) * LANES] for s in range(4)]
        here = v[0] + one_column(v[1])
        late = pltpu.roll(v[2] + one_column(v[3]), half, 1)
        pieces.append(here + jnp.where(first_row, carry, late))
        carry = late
    return jnp.concatenate(pieces, axis=1), carry


def own_kernel(dims, vol, filt, x_hi, x_lo, part, w_halo, w_back, w_spill, w_t):
    chans, outs, planes, height, half = dims
    w_t[...] = jnp.zeros_like(w_t)
    for p in range(3):
        for q in range(3):
            for r in range(3):
                (rho, sb), (gamma, sc) = PLACE[q], PLACE[r]
                top = ((p * 2 + rho) * 2 + gamma) * chans
                left = (sb * 2 + sc) * outs
                tap = (p * 3 + q) * 3 + r
                w_t[top : top + chans, left : left + outs] = filt[tap * chans : (tap + 1) * chans, :]
    edge = 4 * chans
    hi, lo = split(w_t[...])
    w_spill[...] = jnp.concatenate([hi[:edge], hi[:edge], lo[:edge]], axis=1)
    w_back[...] = jnp.concatenate([hi[edge:], hi[edge:], lo[edge:]], axis=1)
    hi, lo = hi.astype(F32), lo.astype(F32)
    w_halo[...] = jnp.concatenate([hi[:edge], hi[:edge], lo[:edge]], axis=0).T.astype(BF16)
    w_own = jnp.concatenate([hi[edge:], hi[edge:], lo[edge:]], axis=0).T.astype(BF16)
    matrix = pairing(half, False)

    def load(plane, row):
        return vol[pl.ds(plane * height + row, chans, stride=planes * height), :]

    def body(step, carry):
        hi, lo = parity_split(load, planes, step, matrix, half)
        cells = pl.ds(pl.multiple_of(step * STEP * LANES, STEP * LANES), STEP * LANES)
        x_hi[:, cells] = hi
        x_lo[:, cells] = lo
        y = jnp.dot(w_own, jnp.concatenate([hi, lo, hi], axis=0), preferred_element_type=F32)
        total, carry = shift_add(y, outs, half, carry)
        part[:, cells] = total
        return carry

    lax.fori_loop(0, height // (4 * STEP), body, jnp.zeros((outs, LANES), F32))


def halo_kernel(dims, own, count, plane, part, w_halo, x_hi, x_lo, *rest):
    chans, outs, planes, height, half = dims
    results, total_ref = rest[:-1], rest[-1]
    matrix = pairing(half, False)
    weights = w_halo[...]

    def load(_, row):
        return plane[pl.ds(row, chans, stride=height), :]

    def body(step, carry):
        hi, lo = parity_split(load, 1, step, matrix, half)
        cells = pl.ds(pl.multiple_of(step * STEP * LANES, STEP * LANES), STEP * LANES)
        x_hi[:, cells] = hi
        x_lo[:, cells] = lo
        y = jnp.dot(weights, jnp.concatenate([hi, lo, hi], axis=0), preferred_element_type=F32)
        total, carry = shift_add(y, outs, half, carry)
        total_ref[:, cells] = part[:, cells] + total
        return carry

    lax.fori_loop(0, height // (4 * STEP), body, jnp.zeros((outs, LANES), F32))
    me = lax.axis_index("chan")
    for k in range(count):
        start = pl.multiple_of(lax.rem(me + k, count) * own, own)
        results[k][...] = total_ref[pl.ds(start, own), :]


def filter_kernel(dims, own, count, *refs):
    chans, outs, planes, height, half = dims
    grads, (x_hi, x_lo, xh_hi, xh_lo) = refs[:count], refs[count : count + 4]
    g_hi, g_lo, packed, g_all, total = refs[count + 4 :]
    cells_all = grads[0].shape[1]
    me = lax.axis_index("chan")
    for k in range(count):
        start = pl.multiple_of(lax.rem(me + count - k, count) * own, own)
        g_all[pl.ds(start, own), :cells_all] = grads[k][...]
    g_all[:, cells_all:] = jnp.zeros((outs, LANES), F32)
    total[...] = jnp.zeros_like(total)
    lane = lane_of((outs, LANES))
    last_column = lane % half == half - 1
    first_row = lane < half

    def one_column(v):
        return jnp.where(last_column, 0.0, pltpu.roll(v, LANES - 1, 1))

    def body(step, _):
        base = step * STEP * LANES
        v = [g_all[:, pl.ds(pl.multiple_of(base + j * LANES, LANES), LANES)] for j in range(STEP + 1)]
        swapped = [pltpu.roll(a, half, 1) for a in v]
        pieces = []
        for j in range(STEP):
            later = jnp.where(first_row, swapped[j], swapped[j + 1])
            pieces.append(jnp.concatenate([v[j], one_column(v[j]), later, one_column(later)], axis=0))
        hi, lo = split(jnp.concatenate(pieces, axis=1))
        cells = pl.ds(pl.multiple_of(base, STEP * LANES), STEP * LANES)
        g_hi[:, cells] = hi
        g_lo[:, cells] = lo
        a_hi = jnp.concatenate([xh_hi[:, cells], x_hi[:, cells]], axis=0)
        a_lo = jnp.concatenate([xh_lo[:, cells], x_lo[:, cells]], axis=0)
        total[...] += lax.dot_general(
            jnp.concatenate([a_hi, a_hi, a_lo], axis=1),
            jnp.concatenate([hi, lo, hi], axis=1),
            (((1,), (1,)), ((), ())),
            preferred_element_type=F32,
        )
        return 0

    lax.fori_loop(0, cells_all // (STEP * LANES), body, 0)

    def tap_block(tap, side):
        p, q, r = tap // 9, tap // 3 % 3, tap % 3
        (rho, sb), (gamma, sc) = PLACE[q], PLACE[r]
        top = ((p * 2 + rho) * 2 + gamma) * chans
        block = total[top : top + chans, sb * LANES : (sb + 1) * LANES]
        return block if sc == side else pltpu.roll(block, outs, 1)

    left_side = lane_of((chans, LANES)) < outs
    for tap in range(14):
        right = tap_block(tap + 14, 1) if tap + 14 < 27 else jnp.zeros((chans, LANES), F32)
        packed[tap * chans : (tap + 1) * chans, :] = jnp.where(left_side, tap_block(tap, 0), right)


def back_kernel(dims, planes, weights, g_hi, g_lo, out):
    chans, outs, _, height, half = dims
    matrix = pairing(half, True)
    matrix = jnp.concatenate([matrix, matrix], axis=0)
    w = weights[...]

    def body(step, _):
        cells = pl.ds(pl.multiple_of(step * STEP * LANES, STEP * LANES), STEP * LANES)
        hi, lo = g_hi[:, cells], g_lo[:, cells]
        grad = jnp.dot(w, jnp.concatenate([hi, lo, hi], axis=0), preferred_element_type=F32)
        tiles = []
        for group in range(planes * 2):
            for j in range(STEP):
                sides = [
                    grad[(group * 2 + column) * chans : (group * 2 + column + 1) * chans, j * LANES : (j + 1) * LANES]
                    for column in range(2)
                ]
                tiles.append(jnp.concatenate(sides, axis=1))
        hi, lo = split(jnp.concatenate(tiles, axis=0))
        rows = jnp.dot(jnp.concatenate([hi, lo], axis=1), matrix, preferred_element_type=F32)
        for group in range(planes * 2):
            for j in range(STEP):
                start = (group * STEP + j) * chans
                row = (group // 2) * height + 4 * (step * STEP + j) + group % 2
                for side in range(2):
                    out[pl.ds(row + 2 * side, chans, stride=planes * height), :] = rows[
                        start : start + chans, side * LANES : (side + 1) * LANES
                    ]
        return 0

    lax.fori_loop(0, height // (4 * STEP), body, 0)


def call(kernel, name, shapes, scratch, *args):
    return pl.pallas_call(
        kernel,
        name=name,
        out_shape=[jax.ShapeDtypeStruct(s, t) for s, t in shapes],
        in_specs=[VMEM] * len(args),
        out_specs=[VMEM] * len(shapes),
        scratch_shapes=scratch,
        compiler_params=pltpu.CompilerParams(vmem_limit_bytes=48 * 1024 * 1024),
    )(*args)


def turned(value, axis, steps):
    count = lax.axis_size(axis)
    return lax.ppermute(value, axis, [(s, (s + steps) % count) for s in range(count)])


def from_behind(value, axis, steps):
    count = lax.axis_size(axis)
    initial, last = (max(0, -steps), min(count, count - steps))
    return lax.ppermute(value, axis, [(source, source + steps) for source in range(initial, last)])


def sum_over(value, axis):
    count = lax.axis_size(axis)
    if count & (count - 1):
        return lax.psum(value, axis)
    bit = 1
    while bit < count:
        value = value + lax.ppermute(value, axis, [(s, s ^ bit) for s in range(count)])
        bit *= 2
    return value


def on_device(volume, filters, cotangent):
    real, planes, height, width = volume.shape
    outs = filters.shape[0]
    own = cotangent.shape[0]
    count = lax.axis_size("chan")
    half = width // 2
    cells = (height // 2) * half
    assert planes == 2 and width == LANES and height % (4 * STEP) == 0 and 2 * outs == LANES
    chans = -(-real // 16) * 16
    taps = filters.transpose(2, 3, 4, 1, 0)
    if chans > real:
        volume = jnp.pad(volume, ((0, chans - real), (0, 0), (0, 0), (0, 0)))
        taps = jnp.pad(taps, ((0, 0), (0, 0), (0, 0), (0, chans - real), (0, 0)))
    dims = (chans, outs, planes, height, half)
    halo = from_behind(volume[:, -1], "space", 1)
    x_hi, x_lo, part, w_halo, w_back, w_spill = call(
        functools.partial(own_kernel, dims),
        "own",
        [
            ((8 * chans, cells), BF16),
            ((8 * chans, cells), BF16),
            ((outs, cells), F32),
            ((4 * outs, 12 * chans), BF16),
            ((8 * chans, 12 * outs), BF16),
            ((4 * chans, 12 * outs), BF16),
        ],
        [pltpu.VMEM((12 * chans, 4 * outs), F32)],
        volume.reshape(chans * planes * height, width),
        taps.reshape(27 * chans, outs),
    )
    xh_hi, xh_lo, *pieces = call(
        functools.partial(halo_kernel, dims, own, count),
        "halo",
        [((4 * chans, cells), BF16)] * 2 + [((own, cells), F32)] * count,
        [pltpu.VMEM((outs, cells), F32)],
        halo.reshape(chans * height, width),
        part,
        w_halo,
    )
    preact = pieces[0]
    for k in range(1, count):
        preact = preact + turned(pieces[k], "chan", k)
    activated = jax.nn.softplus(preact).reshape(cotangent.shape)
    grad = cotangent.reshape(own, cells) * jax.nn.sigmoid(preact)
    grads = [grad] + [turned(grad, "chan", k) for k in range(1, count)]
    g_hi, g_lo, packed = call(
        functools.partial(filter_kernel, dims, own, count),
        "filter",
        [((4 * outs, cells), BF16)] * 2 + [((14 * chans, LANES), F32)],
        [pltpu.VMEM((outs, cells + LANES), F32), pltpu.VMEM((12 * chans, 4 * outs), F32)],
        *grads,
        x_hi,
        x_lo,
        xh_hi,
        xh_lo,
    )
    packed = sum_over(packed, "space")
    (spill,) = call(
        functools.partial(back_kernel, dims, 1), "spill", [((chans * height, width), F32)], [], w_spill, g_hi, g_lo
    )
    spilled = from_behind(spill, "space", -1)
    (volume_grad,) = call(
        functools.partial(back_kernel, dims, 2), "back", [((chans * 2 * height, width), F32)], [], w_back, g_hi, g_lo
    )
    volume_grad = volume_grad.reshape(chans, planes, height, width)
    volume_grad = volume_grad.at[:, -1].add(spilled.reshape(chans, height, width))[:real]
    depth_all = planes * lax.axis_size("space")
    factor = float(depth_all // 2 * (height // 2) * half) ** (-0.5)
    unpacked = jnp.concatenate([packed[:, :outs], packed[: 13 * chans, outs:]], axis=0) * factor
    filter_grad = unpacked.reshape(3, 3, 3, chans, outs)[:, :, :, :real].transpose(4, 3, 0, 1, 2)
    return (activated, volume_grad, filter_grad)


def solution(mesh):
    in_specs = (
        P("chan", "space", None, None),
        P(None, "chan", None, None, None),
        P("chan", "space", None, None),
    )
    out_specs = (
        P("chan", "space", None, None),
        P("chan", "space", None, None),
        P(None, "chan", None, None, None),
    )
    return jax.shard_map(
        on_device, mesh=mesh, in_specs=in_specs, out_specs=out_specs, check_vma=False
    )
```

```python
import functools

import jax
import jax.numpy as jnp
from jax import lax
from jax.experimental import pallas as pl
from jax.experimental.pallas import tpu as pltpu
from jax.sharding import PartitionSpec as P

F32 = jnp.float32
BF16 = jnp.bfloat16
LANES = 128
STEP = 8
CHUNKS = 2
VMEM = pl.BlockSpec(memory_space=pltpu.VMEM)
ANY = pl.BlockSpec(memory_space=pl.ANY)

PLACE = {0: (1, 1), 1: (0, 0), 2: (1, 0)}


def split(x):
    hi = x.astype(BF16)
    return hi, (x - hi.astype(F32)).astype(BF16)


def pairing(half, transposed):
    size = 4 * half
    cell = lax.broadcasted_iota(jnp.int32, (size, size), 0 if transposed else 1)
    source = lax.broadcasted_iota(jnp.int32, (size, size), 1 if transposed else 0)
    parity, rest = cell // (2 * half), cell % (2 * half)
    wanted = (rest // half) * (2 * half) + 2 * (rest % half) + parity
    return (source == wanted).astype(F32).astype(BF16)


def lane_of(shape):
    return lax.broadcasted_iota(jnp.int32, shape, 1)


def group(index, count=1):
    return slice(index * LANES, (index + count) * LANES)


def parity_split(load, planes, first, matrix):
    tiles = []
    for plane in range(planes):
        for parity in range(2):
            for j in range(STEP):
                row = 4 * (first + j) + parity
                tiles.append(jnp.concatenate([load(plane, row), load(plane, row + 2)], axis=1))
    chans = tiles[0].shape[0]
    hi, lo = split(jnp.concatenate(tiles, axis=0))
    moved = jnp.dot(jnp.concatenate([hi, lo], axis=0), matrix, preferred_element_type=F32).astype(BF16)
    parts = []
    for part in range(2):
        rows = []
        for parity in range(planes * 2):
            for column in range(2):
                pieces = []
                for j in range(STEP):
                    start = ((part * planes * 2 + parity) * STEP + j) * chans
                    pieces.append(moved[start : start + chans, group(column)])
                rows.append(jnp.concatenate(pieces, axis=1))
        parts.append(jnp.concatenate(rows, axis=0))
    return parts


def shift_add(y, outs, half, carry):
    lane = lane_of((outs, LANES))
    first_column = lane % half == 0
    first_row = lane < half

    def one_column(v):
        return jnp.where(first_column, 0.0, pltpu.roll(v, 1, 1))

    pieces = []
    for j in range(STEP):
        v = [y[s * outs : (s + 1) * outs, group(j)] for s in range(4)]
        here = v[0] + one_column(v[1])
        late = pltpu.roll(v[2] + one_column(v[3]), half, 1)
        pieces.append(here + jnp.where(first_row, carry, late))
        carry = late
    return jnp.concatenate(pieces, axis=1), carry


def grad_shifts(load, first, count, outs, half):
    lane = lane_of((outs, LANES))
    last_column = lane % half == half - 1
    first_row = lane < half

    def one_column(v):
        return jnp.where(last_column, 0.0, pltpu.roll(v, LANES - 1, 1))

    v = [load(first + j) for j in range(count + 1)]
    swapped = [pltpu.roll(a, half, 1) for a in v]
    pieces = []
    for j in range(count):
        later = jnp.where(first_row, swapped[j], swapped[j + 1])
        pieces.append(jnp.concatenate([v[j], one_column(v[j]), later, one_column(later)], axis=0))
    return split(jnp.concatenate(pieces, axis=1))


def gather_grads(pieces, scratch, own, count):
    me = lax.axis_index("chan")
    left = 0
    for chunk in range(len(pieces) // count):
        for k in range(count):
            piece = pieces[chunk * count + k]
            start = pl.multiple_of(lax.rem(me + count - k, count) * own, own)
            scratch[pl.ds(start, own), left : left + piece.shape[1]] = piece[...]
        left += piece.shape[1]
    if left < scratch.shape[1]:
        scratch[:, left:] = jnp.zeros((scratch.shape[0], scratch.shape[1] - left), F32)


def own_kernel(dims, vol, filt, x_hi, x_lo, part, w_halo, w_back, w_next, w_t):
    chans, outs, planes, height, half = dims
    w_t[...] = jnp.zeros_like(w_t)
    for p in range(3):
        for q in range(3):
            for r in range(3):
                (rho, sb), (gamma, sc) = PLACE[q], PLACE[r]
                top = ((p * 2 + rho) * 2 + gamma) * chans
                left = (sb * 2 + sc) * outs
                tap = (p * 3 + q) * 3 + r
                w_t[top : top + chans, left : left + outs] = filt[tap * chans : (tap + 1) * chans, :]
    edge = 4 * chans
    hi, lo = split(w_t[...])
    w_next[...] = jnp.concatenate([hi[:edge], hi[:edge], lo[:edge]], axis=1)
    w_back[...] = jnp.concatenate([hi[edge:], hi[edge:], lo[edge:]], axis=1)
    hi, lo = hi.astype(F32), lo.astype(F32)
    w_halo[...] = jnp.concatenate([hi[:edge], hi[:edge], lo[:edge]], axis=0).T.astype(BF16)
    w_own = jnp.concatenate([hi[edge:], hi[edge:], lo[edge:]], axis=0).T.astype(BF16)
    matrix = pairing(half, False)

    def load(plane, row):
        return vol[pl.ds(plane * height + row, chans, stride=planes * height), :]

    carry = jnp.zeros((outs, LANES), F32)
    for first in range(0, height // 4, STEP):
        hi, lo = parity_split(load, planes, first, matrix)
        cells = group(first, STEP)
        x_hi[:, cells] = hi
        x_lo[:, cells] = lo
        y = jnp.dot(w_own, jnp.concatenate([hi, lo, hi], axis=0), preferred_element_type=F32)
        part[:, cells], carry = shift_add(y, outs, half, carry)


def halo_kernel(dims, own, count, chunk, *refs):
    chans, outs, planes, height, half = dims
    plane, part, w_halo = refs[:3]
    before = refs[3] if chunk else None
    x_hi, x_lo, *results, total = refs[4 if chunk else 3 :]
    after = results[count] if len(results) > count else None
    matrix = pairing(half, False)
    weights = w_halo[...]
    rows = height // CHUNKS

    def load(_, row):
        return plane[pl.ds(row, chans, stride=rows), :]

    carry = before[...] if chunk else jnp.zeros((outs, LANES), F32)
    for first in range(0, rows // 4, STEP):
        hi, lo = parity_split(load, 1, first, matrix)
        cells = group(first, STEP)
        x_hi[:, cells] = hi
        x_lo[:, cells] = lo
        y = jnp.dot(weights, jnp.concatenate([hi, lo, hi], axis=0), preferred_element_type=F32)
        added, carry = shift_add(y, outs, half, carry)
        total[:, cells] = part[:, group(chunk * (rows // 4) + first, STEP)] + added
    if after is not None:
        after[...] = carry
    me = lax.axis_index("chan")
    for k in range(count):
        start = pl.multiple_of(lax.rem(me + k, count) * own, own)
        results[k][...] = total[pl.ds(start, own), :]


def filter_kernel(dims, own, count, chunk, *refs):
    chans, outs, planes, height, half = dims
    per = height // 4 // CHUNKS
    loaded = min(chunk, 1) + 1
    last = chunk == CHUNKS - 1
    pieces, refs = refs[: loaded * count], refs[loaded * count :]
    (x_hi, x_lo), refs = refs[:2], refs[2:]
    halos, refs = refs[: 2 * loaded], refs[2 * loaded :]
    if chunk:
        before, refs = refs[0], refs[1:]
    out, total, g_all = refs
    gather_grads(pieces, g_all, own, count)
    base = (chunk - loaded + 1) * per
    begin = chunk * per - (1 if chunk else 0)
    end = (chunk + 1) * per - (0 if last else 1)
    total[...] = before[...] if chunk else jnp.zeros_like(total)

    def halo_part(part, first, size):
        found = []
        for h in range(loaded):
            low = max(first - base, h * per)
            high = min(first - base + size, (h + 1) * per)
            if low < high:
                found.append(halos[2 * h + part][:, group(low - h * per, high - low)])
        return found[0] if len(found) == 1 else jnp.concatenate(found, axis=1)

    first = begin
    while first < end:
        size = min(STEP, end - first)
        hi, lo = grad_shifts(lambda g: g_all[:, group(g - base)], first, size, outs, half)
        a_hi = jnp.concatenate([halo_part(0, first, size), x_hi[:, group(first, size)]], axis=0)
        a_lo = jnp.concatenate([halo_part(1, first, size), x_lo[:, group(first, size)]], axis=0)
        total[...] += lax.dot_general(
            jnp.concatenate([a_hi, a_hi, a_lo], axis=1),
            jnp.concatenate([hi, lo, hi], axis=1),
            (((1,), (1,)), ((), ())),
            preferred_element_type=F32,
        )
        first += size
    if not last:
        out[...] = total[...]
        return

    def tap_block(tap, side):
        p, q, r = tap // 9, tap // 3 % 3, tap % 3
        (rho, sb), (gamma, sc) = PLACE[q], PLACE[r]
        top = ((p * 2 + rho) * 2 + gamma) * chans
        block = total[top : top + chans, group(sb)]
        return block if sc == side else pltpu.roll(block, outs, 1)

    left_side = lane_of((chans, LANES)) < outs
    for tap in range(14):
        right = tap_block(tap + 14, 1) if tap + 14 < 27 else jnp.zeros((chans, LANES), F32)
        out[tap * chans : (tap + 1) * chans, :] = jnp.where(left_side, tap_block(tap, 0), right)


def back_kernel(dims, own, count, depth, *refs):
    chans, outs, planes, height, half = dims
    total = count * CHUNKS
    here, refs = refs[:total], refs[total:]
    if depth:
        above, w_next, refs = refs[:total], refs[total], refs[total + 1 :]
    weights, refs = refs[0], refs[1:]
    out, g_here, plane, sem = refs[-5 if depth else -4], refs[-4 if depth else -3], refs[-2], refs[-1]
    gather_grads(here, g_here, own, count)
    if depth:
        g_above = refs[-3]
        gather_grads(above, g_above, own, count)
        w_above = w_next[...]
    matrix = pairing(half, True)
    matrix = jnp.concatenate([matrix, matrix], axis=0)
    w_here = weights[depth * 4 * chans : (depth + 1) * 4 * chans, :]
    for first in range(0, height // 4, STEP):
        hi, lo = grad_shifts(lambda g: g_here[:, group(g)], first, STEP, outs, half)
        grad = jnp.dot(w_here, jnp.concatenate([hi, lo, hi], axis=0), preferred_element_type=F32)
        if depth:
            hi, lo = grad_shifts(lambda g: g_above[:, group(g)], first, STEP, outs, half)
            grad += jnp.dot(w_above, jnp.concatenate([hi, lo, hi], axis=0), preferred_element_type=F32)
        tiles = []
        for parity in range(2):
            for j in range(STEP):
                tops = [(parity * 2 + column) * chans for column in range(2)]
                tiles.append(jnp.concatenate([grad[t : t + chans, group(j)] for t in tops], axis=1))
        hi, lo = split(jnp.concatenate(tiles, axis=0))
        rows = jnp.dot(jnp.concatenate([hi, lo], axis=1), matrix, preferred_element_type=F32)
        for parity in range(2):
            for j in range(STEP):
                start = (parity * STEP + j) * chans
                row = 4 * (first + j) + parity
                for side in range(2):
                    plane[pl.ds(row + 2 * side, chans, stride=height), :] = rows[
                        start : start + chans, group(side)
                    ]
    copies = []
    for i in range(chans):
        source = plane.at[pl.ds(i * height, height), :]
        target = out.at[pl.ds((i * planes + depth) * height, height), :]
        copies.append(pltpu.make_async_copy(source, target, sem.at[i]))
        copies[-1].start()
    for copy in copies:
        copy.wait()


def flat_kernel(half, cube, flat):
    own, cells = flat.shape
    for g in range(cells // LANES):
        sides = [cube[pl.ds(2 * g + side, own, stride=cells // half), :] for side in range(2)]
        flat[:, group(g)] = jnp.concatenate(sides, axis=1)


def activation_kernel(half, *refs):
    *chunks, cube = refs
    own, cells = chunks[0].shape
    for h, chunk in enumerate(chunks):
        for g in range(cells // LANES):
            x = chunk[:, group(g)]
            value = jnp.maximum(x, 0.0) + jnp.log1p(jnp.exp(-jnp.abs(x)))
            row = 2 * (h * (cells // LANES) + g)
            stride = len(chunks) * cells // half
            cube[pl.ds(row, own, stride=stride), :] = value[:, :half]
            cube[pl.ds(row + 1, own, stride=stride), :] = value[:, half:]


def call(kernel, name, time, shapes, scratch, *args, in_place=False):
    specs = [VMEM] * len(args)
    if in_place:
        specs[-1] = ANY
    return pl.pallas_call(
        kernel,
        name=name,
        out_shape=[jax.ShapeDtypeStruct(s, t) for s, t in shapes],
        in_specs=specs,
        out_specs=[ANY if name.startswith("back") else VMEM] * len(shapes),
        scratch_shapes=scratch,
        input_output_aliases={len(args) - 1: 0} if in_place else {},
        cost_estimate=pl.CostEstimate(flops=0, bytes_accessed=int(time * 3.6e6), transcendentals=0),
        compiler_params=pltpu.CompilerParams(vmem_limit_bytes=12 * 1024 * 1024),
    )(*args)


def turned(value, axis, steps):
    count = lax.axis_size(axis)
    return lax.ppermute(value, axis, [(s, (s + steps) % count) for s in range(count)])


def from_behind(value, axis, steps):
    count = lax.axis_size(axis)
    initial, last = (max(0, -steps), min(count, count - steps))
    return lax.ppermute(value, axis, [(source, source + steps) for source in range(initial, last)])


def sum_over(value, axis, beside):
    count = lax.axis_size(axis)
    if count & (count - 1):
        return beside(0, lax.psum(value, axis))
    bit = 1
    while bit < count:
        value = value + lax.ppermute(value, axis, [(s, s ^ bit) for s in range(count)])
        value = beside(bit.bit_length() - 1, value)
        bit *= 2
    return value


def on_device(volume, filters, cotangent):
    real, planes, height, width = volume.shape
    outs = filters.shape[0]
    own = cotangent.shape[0]
    count = lax.axis_size("chan")
    half = width // 2
    cells = (height // 2) * half
    part_cells = cells // CHUNKS
    assert planes == 2 and width == LANES and height % (4 * STEP * CHUNKS) == 0 and 2 * outs == LANES
    chans = -(-real // 16) * 16
    taps = filters.transpose(2, 3, 4, 1, 0)
    if chans > real:
        volume = jnp.pad(volume, ((0, chans - real), (0, 0), (0, 0), (0, 0)))
        taps = jnp.pad(taps, ((0, 0), (0, 0), (0, 0), (0, chans - real), (0, 0)))
    dims = (chans, outs, planes, height, half)
    rows = height // CHUNKS
    halos = [from_behind(volume[:, -1, h * rows : (h + 1) * rows], "space", 1) for h in range(CHUNKS)]
    x_hi, x_lo, part, w_halo, w_back, w_next = call(
        functools.partial(own_kernel, dims),
        "own",
        3.5,
        [
            ((8 * chans, cells), BF16),
            ((8 * chans, cells), BF16),
            ((outs, cells), F32),
            ((4 * outs, 12 * chans), BF16),
            ((8 * chans, 12 * outs), BF16),
            ((4 * chans, 12 * outs), BF16),
        ],
        [pltpu.VMEM((12 * chans, 4 * outs), F32)],
        volume.reshape(chans * planes * height, width),
        taps.reshape(27 * chans, outs),
    )
    (upstream,) = call(
        functools.partial(flat_kernel, half), "flat", 0.8, [((own, cells), F32)], [], cotangent.reshape(-1, half)
    )
    x_halos, preacts, grads, carry = [], [], [], []
    for h in range(CHUNKS):
        shapes = [((4 * chans, part_cells), BF16)] * 2 + [((own, part_cells), F32)] * count
        if h < CHUNKS - 1:
            shapes.append(((outs, LANES), F32))
        xh_hi, xh_lo, *pieces = call(
            functools.partial(halo_kernel, dims, own, count, h),
            "halo",
            1.7,
            shapes,
            [pltpu.VMEM((outs, part_cells), F32)],
            halos[h].reshape(chans * rows, width),
            part,
            w_halo,
            *carry,
        )
        x_halos += [xh_hi, xh_lo]
        carry = pieces[count:]
        preact = pieces[0]
        if h:
            preact, _ = lax.optimization_barrier((preact, grads[-1][0]))
        for k in range(1, count):
            preact = preact + turned(pieces[k], "chan", k)
        grad = upstream[:, h * part_cells : (h + 1) * part_cells] * jax.nn.sigmoid(preact)
        preacts.append(preact)
        grads.append([grad] + [turned(grad, "chan", k) for k in range(1, count)])
    above = [[from_behind(g, "space", -1) for g in chunk] for chunk in grads]
    (activated,) = call(
        functools.partial(activation_kernel, half), "activation", 1.2, [((own * (height // 2), half), F32)], [], *preacts
    )
    grads[0][0], activated = lax.optimization_barrier((grads[0][0], activated))

    summed = []
    for h in range(CHUNKS):
        low = max(h - 1, 0)
        last = h == CHUNKS - 1
        if last:
            early = [g for chunk in above[:-1] for g in chunk] + above[-1][:1]
            *early, summed_before = lax.optimization_barrier((*early, summed[0]))
            above = [early[i * count : (i + 1) * count] for i in range(CHUNKS - 1)] + [early[-1:] + above[-1][1:]]
            summed = [summed_before]
        (result,) = call(
            functools.partial(filter_kernel, dims, own, count, h),
            "filter",
            1.6,
            [((14 * chans, LANES) if last else (12 * chans, 4 * outs), F32)],
            [
                pltpu.VMEM((12 * chans, 4 * outs), F32),
                pltpu.VMEM((outs, (h - low + 1) * part_cells + (LANES if last else 0)), F32),
            ],
            *sum(grads[low : h + 1], []),
            x_hi,
            x_lo,
            *x_halos[2 * low : 2 * h + 2],
            *summed,
        )
        summed = [result]
    buffers = [
        pltpu.VMEM((outs, cells + LANES), F32),
        pltpu.VMEM((chans * height, width), F32),
        pltpu.SemaphoreType.DMA((chans,)),
    ]
    shape = [((chans * planes * height, width), F32)]
    state = {}

    def back_work(index, value):
        if index == 0:
            *late, value = lax.optimization_barrier((*above[-1][1:], value))
            above[-1][1:] = late
            sources = sum(grads, [])
            *sources, value = lax.optimization_barrier((*sources, value))
            state["sources"] = sources
            (state["grad"],) = call(
                functools.partial(back_kernel, dims, own, count, 0), "back_0", 3.0, shape, buffers, *sources, w_back
            )
        elif index == 1:
            state["grad"], value = lax.optimization_barrier((state["grad"], value))
        return value

    packed = sum_over(summed[0], "space", back_work)
    (volume_grad,) = call(
        functools.partial(back_kernel, dims, own, count, 1),
        "back_1",
        4.0,
        shape,
        [buffers[0]] + buffers,
        *state["sources"],
        *sum(above, []),
        w_next,
        w_back,
        state["grad"],
        in_place=True,
    )
    volume_grad = volume_grad.reshape(chans, planes, height, width)[:real]
    depth_all = planes * lax.axis_size("space")
    factor = float(depth_all // 2 * (height // 2) * half) ** (-0.5)
    unpacked = jnp.concatenate([packed[:, :outs], packed[: 13 * chans, outs:]], axis=0) * factor
    filter_grad = unpacked.reshape(3, 3, 3, chans, outs)[:, :, :, :real].transpose(4, 3, 0, 1, 2)
    return (activated.reshape(cotangent.shape), volume_grad, filter_grad)


def solution(mesh):
    in_specs = (
        P("chan", "space", None, None),
        P(None, "chan", None, None, None),
        P("chan", "space", None, None),
    )
    out_specs = (
        P("chan", "space", None, None),
        P("chan", "space", None, None),
        P(None, "chan", None, None, None),
    )
    return jax.shard_map(
        on_device, mesh=mesh, in_specs=in_specs, out_specs=out_specs, check_vma=False
    )
```

```python
import functools

import jax
import jax.numpy as jnp
from jax import lax
from jax.experimental import pallas as pl
from jax.experimental.pallas import tpu as pltpu
from jax.sharding import PartitionSpec as P

F32 = jnp.float32
BF16 = jnp.bfloat16
LANES = 128
STEP = 8
CHUNKS = 2
BACK = (10, 22)
VMEM = pl.BlockSpec(memory_space=pltpu.VMEM)
ANY = pl.BlockSpec(memory_space=pl.ANY)

PLACE = {0: (1, 1), 1: (0, 0), 2: (1, 0)}


def split(x):
    hi = x.astype(BF16)
    return hi, (x - hi.astype(F32)).astype(BF16)


def pairing(half, transposed):
    size = 4 * half
    cell = lax.broadcasted_iota(jnp.int32, (size, size), 0 if transposed else 1)
    source = lax.broadcasted_iota(jnp.int32, (size, size), 1 if transposed else 0)
    parity, rest = cell // (2 * half), cell % (2 * half)
    wanted = (rest // half) * (2 * half) + 2 * (rest % half) + parity
    return (source == wanted).astype(F32).astype(BF16)


def lane_of(shape):
    return lax.broadcasted_iota(jnp.int32, shape, 1)


def group(index, count=1):
    return slice(index * LANES, (index + count) * LANES)


def parity_split(load, planes, first, matrix):
    tiles = []
    for plane in range(planes):
        for parity in range(2):
            for j in range(STEP):
                row = 4 * (first + j) + parity
                tiles.append(jnp.concatenate([load(plane, row), load(plane, row + 2)], axis=1))
    chans = tiles[0].shape[0]
    hi, lo = split(jnp.concatenate(tiles, axis=0))
    moved = jnp.dot(jnp.concatenate([hi, lo], axis=0), matrix, preferred_element_type=F32).astype(BF16)
    parts = []
    for part in range(2):
        rows = []
        for parity in range(planes * 2):
            for column in range(2):
                pieces = []
                for j in range(STEP):
                    start = ((part * planes * 2 + parity) * STEP + j) * chans
                    pieces.append(moved[start : start + chans, group(column)])
                rows.append(jnp.concatenate(pieces, axis=1))
        parts.append(jnp.concatenate(rows, axis=0))
    return parts


def shift_add(y, outs, half, carry):
    lane = lane_of((outs, LANES))
    first_column = lane % half == 0
    first_row = lane < half

    def one_column(v):
        return jnp.where(first_column, 0.0, pltpu.roll(v, 1, 1))

    pieces = []
    for j in range(STEP):
        v = [y[s * outs : (s + 1) * outs, group(j)] for s in range(4)]
        here = v[0] + one_column(v[1])
        late = pltpu.roll(v[2] + one_column(v[3]), half, 1)
        pieces.append(here + jnp.where(first_row, carry, late))
        carry = late
    return jnp.concatenate(pieces, axis=1), carry


def grad_shifts(load, first, count, outs, half):
    lane = lane_of((outs, LANES))
    last_column = lane % half == half - 1
    first_row = lane < half

    def one_column(v):
        return jnp.where(last_column, 0.0, pltpu.roll(v, LANES - 1, 1))

    v = [load(first + j) for j in range(count + 1)]
    swapped = [pltpu.roll(a, half, 1) for a in v]
    pieces = []
    for j in range(count):
        later = jnp.where(first_row, swapped[j], swapped[j + 1])
        pieces.append(jnp.concatenate([v[j], one_column(v[j]), later, one_column(later)], axis=0))
    return split(jnp.concatenate(pieces, axis=1))


def gather_grads(pieces, scratch, own, count):
    me = lax.axis_index("chan")
    left = 0
    for chunk in range(len(pieces) // count):
        for k in range(count):
            piece = pieces[chunk * count + k]
            start = pl.multiple_of(lax.rem(me + count - k, count) * own, own)
            scratch[pl.ds(start, own), left : left + piece.shape[1]] = piece[...]
        left += piece.shape[1]
    if left < scratch.shape[1]:
        scratch[:, left:] = jnp.zeros((scratch.shape[0], scratch.shape[1] - left), F32)


def own_kernel(dims, chunk, vol, *refs):
    chans, outs, planes, height, half = dims
    rows = height // CHUNKS
    if chunk:
        w_own, before = refs[:2]
        x_hi, x_lo, part, *rest = refs[2:]
        carry, weights = before[...], w_own[...]
        after = rest[0] if rest else None
    else:
        filt, x_hi, x_lo, part, w_own, w_halo, w_back, after, w_t = refs
        carry, weights = jnp.zeros((outs, LANES), F32), lay_weights(dims, filt, w_t, w_own, w_halo, w_back)
    matrix = pairing(half, False)

    def load(plane, row):
        return vol[pl.ds(plane * height + chunk * rows + row, chans, stride=planes * height), :]

    for first in range(0, rows // 4, STEP):
        hi, lo = parity_split(load, planes, first, matrix)
        cells = group(first, STEP)
        x_hi[:, cells] = hi
        x_lo[:, cells] = lo
        y = jnp.dot(weights, jnp.concatenate([hi, lo, hi], axis=0), preferred_element_type=F32)
        part[:, cells], carry = shift_add(y, outs, half, carry)
    if after is not None:
        after[...] = carry


def lay_weights(dims, filt, w_t, w_own, w_halo, w_back):
    chans, outs, planes, height, half = dims
    w_t[...] = jnp.zeros_like(w_t)
    for p in range(3):
        for q in range(3):
            for r in range(3):
                (rho, sb), (gamma, sc) = PLACE[q], PLACE[r]
                top = ((p * 2 + rho) * 2 + gamma) * chans
                left = (sb * 2 + sc) * outs
                tap = (p * 3 + q) * 3 + r
                w_t[top : top + chans, left : left + outs] = filt[tap * chans : (tap + 1) * chans, :]
    edge = 4 * chans
    hi, lo = split(w_t[...])
    here = jnp.concatenate([hi[edge:], hi[edge:], lo[edge:]], axis=1)
    above = jnp.concatenate([hi[:edge], hi[:edge], lo[:edge]], axis=1)
    w_back[...] = jnp.concatenate([here, jnp.concatenate([jnp.zeros_like(above), above], axis=0)], axis=1)
    hi, lo = hi.astype(F32), lo.astype(F32)
    w_halo[...] = jnp.concatenate([hi[:edge], hi[:edge], lo[:edge]], axis=0).T.astype(BF16)
    hi, lo = split(w_t[edge:, :].T)
    weights = jnp.concatenate([hi, hi, lo], axis=1)
    w_own[...] = weights
    return weights


def halo_kernel(dims, own, count, chunk, *refs):
    chans, outs, planes, height, half = dims
    plane, part, w_halo = refs[:3]
    before = refs[3] if chunk else None
    x_hi, x_lo, *results, total = refs[4 if chunk else 3 :]
    after = results[count] if len(results) > count else None
    matrix = pairing(half, False)
    weights = w_halo[...]
    rows = height // CHUNKS

    def load(_, row):
        return plane[pl.ds(row, chans, stride=rows), :]

    carry = before[...] if chunk else jnp.zeros((outs, LANES), F32)
    for first in range(0, rows // 4, STEP):
        hi, lo = parity_split(load, 1, first, matrix)
        cells = group(first, STEP)
        x_hi[:, cells] = hi
        x_lo[:, cells] = lo
        y = jnp.dot(weights, jnp.concatenate([hi, lo, hi], axis=0), preferred_element_type=F32)
        added, carry = shift_add(y, outs, half, carry)
        total[:, cells] = part[:, cells] + added
    if after is not None:
        after[...] = carry
    me = lax.axis_index("chan")
    for k in range(count):
        start = pl.multiple_of(lax.rem(me + k, count) * own, own)
        results[k][...] = total[pl.ds(start, own), :]


def filter_kernel(dims, own, count, chunk, *refs):
    chans, outs, planes, height, half = dims
    per = height // 4 // CHUNKS
    loaded = min(chunk, 1) + 1
    last = chunk == CHUNKS - 1
    pieces, refs = refs[: loaded * count], refs[loaded * count :]
    planes_x, refs = refs[: 2 * loaded], refs[2 * loaded :]
    halos, refs = refs[: 2 * loaded], refs[2 * loaded :]
    if chunk:
        before, refs = refs[0], refs[1:]
    out, total, g_all = refs
    gather_grads(pieces, g_all, own, count)
    base = (chunk - loaded + 1) * per
    begin = chunk * per - (1 if chunk else 0)
    end = (chunk + 1) * per - (0 if last else 1)
    total[...] = before[...] if chunk else jnp.zeros_like(total)

    def cells_of(sources, part, first, size):
        found = []
        for h in range(loaded):
            low = max(first - base, h * per)
            high = min(first - base + size, (h + 1) * per)
            if low < high:
                found.append(sources[2 * h + part][:, group(low - h * per, high - low)])
        return found[0] if len(found) == 1 else jnp.concatenate(found, axis=1)

    first = begin
    while first < end:
        size = min(STEP, end - first)
        hi, lo = grad_shifts(lambda g: g_all[:, group(g - base)], first, size, outs, half)
        a_hi, a_lo = [
            jnp.concatenate([cells_of(v, part, first, size) for v in (halos, planes_x)], axis=0) for part in range(2)
        ]
        total[...] += lax.dot_general(
            jnp.concatenate([a_hi, a_hi, a_lo], axis=1),
            jnp.concatenate([hi, lo, hi], axis=1),
            (((1,), (1,)), ((), ())),
            preferred_element_type=F32,
        )
        first += size
    if not last:
        out[...] = total[...]
        return

    def tap_block(tap, side):
        p, q, r = tap // 9, tap // 3 % 3, tap % 3
        (rho, sb), (gamma, sc) = PLACE[q], PLACE[r]
        top = ((p * 2 + rho) * 2 + gamma) * chans
        block = total[top : top + chans, group(sb)]
        return block if sc == side else pltpu.roll(block, outs, 1)

    left_side = lane_of((chans, LANES)) < outs
    for tap in range(14):
        right = tap_block(tap + 14, 1) if tap + 14 < 27 else jnp.zeros((chans, LANES), F32)
        out[tap * chans : (tap + 1) * chans, :] = jnp.where(left_side, tap_block(tap, 0), right)


def back_kernel(dims, own, count, begin, end, low, high, *refs):
    chans, outs, planes, height, half = dims
    loaded = high - low
    here, above = refs[: loaded * count], refs[loaded * count : 2 * loaded * count]
    weights = refs[2 * loaded * count][...]
    out, g_here, g_above, grown, sem = refs[-5:]
    gather_grads(here, g_here, own, count)
    gather_grads(above, g_above, own, count)
    base = low * (height // 4 // CHUNKS)
    matrix = pairing(half, True)
    matrix = jnp.concatenate([matrix, matrix], axis=0)
    first = begin
    while first < end:
        size = min(STEP, end - first)
        hi, lo = grad_shifts(lambda g: g_here[:, group(g - base)], first, size, outs, half)
        hi_above, lo_above = grad_shifts(lambda g: g_above[:, group(g - base)], first, size, outs, half)
        grad = jnp.dot(
            weights,
            jnp.concatenate([hi, lo, hi, hi_above, lo_above, hi_above], axis=0),
            preferred_element_type=F32,
        )
        tiles = []
        for parity in range(planes * 2):
            for j in range(size):
                tops = [(parity * 2 + column) * chans for column in range(2)]
                tiles.append(jnp.concatenate([grad[t : t + chans, group(j)] for t in tops], axis=1))
        hi, lo = split(jnp.concatenate(tiles, axis=0))
        rows = jnp.dot(jnp.concatenate([hi, lo], axis=1), matrix, preferred_element_type=F32)
        for parity in range(planes * 2):
            for j in range(size):
                start = (parity * size + j) * chans
                row = (parity // 2) * height + 4 * (first + j) + parity % 2
                for side in range(2):
                    grown[pl.ds(row + 2 * side, chans, stride=planes * height), :] = rows[
                        start : start + chans, group(side)
                    ]
        first += size
    copies = []
    for i in range(chans * planes):
        part = pl.ds(i * height + 4 * begin, 4 * (end - begin))
        copies.append(pltpu.make_async_copy(grown.at[part, :], out.at[part, :], sem.at[i]))
        copies[-1].start()
    for copy in copies:
        copy.wait()


def flat_kernel(half, cube, flat):
    own, cells = flat.shape
    for g in range(cells // LANES):
        sides = [cube[pl.ds(2 * g + side, own, stride=cells // half), :] for side in range(2)]
        flat[:, group(g)] = jnp.concatenate(sides, axis=1)


def activation_kernel(half, h, chunk, *refs):
    out, cube, sem = refs[-3:]
    own, cells = chunk.shape
    rows = cells // half
    for g in range(cells // LANES):
        x = chunk[:, group(g)]
        value = jnp.maximum(x, 0.0) + jnp.log1p(jnp.exp(-jnp.abs(x)))
        cube[pl.ds(2 * g, own, stride=rows), :] = value[:, :half]
        cube[pl.ds(2 * g + 1, own, stride=rows), :] = value[:, half:]
    copies = []
    for i in range(own):
        target = out.at[pl.ds((i * CHUNKS + h) * rows, rows), :]
        copies.append(pltpu.make_async_copy(cube.at[pl.ds(i * rows, rows), :], target, sem.at[i]))
        copies[-1].start()
    for copy in copies:
        copy.wait()


def call(kernel, name, time, shapes, scratch, *args, in_place=False):
    specs = [VMEM] * len(args)
    if in_place:
        specs[-1] = ANY
    return pl.pallas_call(
        kernel,
        name=name,
        out_shape=[jax.ShapeDtypeStruct(s, t) for s, t in shapes],
        in_specs=specs,
        out_specs=[ANY if name in ("back", "activation") else VMEM] * len(shapes),
        scratch_shapes=scratch,
        input_output_aliases={len(args) - 1: 0} if in_place else {},
        cost_estimate=pl.CostEstimate(flops=0, bytes_accessed=int(time * 3.6e2), transcendentals=0),
        compiler_params=pltpu.CompilerParams(vmem_limit_bytes=12 * 1024 * 1024),
    )(*args)


def turned(value, axis, steps):
    count = lax.axis_size(axis)
    return lax.ppermute(value, axis, [(s, (s + steps) % count) for s in range(count)])


def from_behind(value, axis, steps):
    count = lax.axis_size(axis)
    initial, last = (max(0, -steps), min(count, count - steps))
    return lax.ppermute(value, axis, [(source, source + steps) for source in range(initial, last)])


def sum_over(value, axis, beside):
    count = lax.axis_size(axis)
    if count & (count - 1):
        return beside(0, lax.psum(value, axis))
    bit = 1
    while bit < count:
        value = value + lax.ppermute(value, axis, [(s, s ^ bit) for s in range(count)])
        value = beside(bit.bit_length() - 1, value)
        bit *= 2
    return value


def on_device(volume, filters, cotangent):
    real, planes, height, width = volume.shape
    outs = filters.shape[0]
    own = cotangent.shape[0]
    count = lax.axis_size("chan")
    half = width // 2
    cells = (height // 2) * half
    part_cells = cells // CHUNKS
    assert planes == 2 and width == LANES and height % (4 * STEP * CHUNKS) == 0 and 2 * outs == LANES
    chans = -(-real // 16) * 16
    taps = filters.transpose(2, 3, 4, 1, 0)
    if chans > real:
        volume = jnp.pad(volume, ((0, chans - real), (0, 0), (0, 0), (0, 0)))
        taps = jnp.pad(taps, ((0, 0), (0, 0), (0, 0), (0, chans - real), (0, 0)))
    dims = (chans, outs, planes, height, half)
    rows = height // CHUNKS
    halos = [from_behind(volume[:, -1, h * rows : (h + 1) * rows], "space", 1) for h in range(CHUNKS)]
    halos = [halo.reshape(chans * rows, width) for halo in halos]
    x_own, parts, before = [], [], []
    for h in range(CHUNKS):
        shapes = [((8 * chans, part_cells), BF16)] * 2 + [((outs, part_cells), F32)]
        carry = [((outs, LANES), F32)] if h < CHUNKS - 1 else []
        if h:
            results = call(
                functools.partial(own_kernel, dims, h), "own", 1.6, shapes + carry, [], volume.reshape(-1, width), w_own, *before
            )
            before = results[3:]
        else:
            results = call(
                functools.partial(own_kernel, dims, h),
                "own",
                2.2,
                shapes
                + [
                    ((4 * outs, 24 * chans), BF16),
                    ((4 * outs, 12 * chans), BF16),
                    ((8 * chans, 24 * outs), BF16),
                    ((outs, LANES), F32),
                ],
                [pltpu.VMEM((12 * chans, 4 * outs), F32)],
                volume.reshape(-1, width),
                taps.reshape(27 * chans, outs),
            )
            w_own, w_halo, w_back, carried = results[3:]
            before = [carried]
        x_own += results[:2]
        parts.append(results[2])
    (upstream,) = call(
        functools.partial(flat_kernel, half), "flat", 0.8, [((own, cells), F32)], [], cotangent.reshape(-1, half)
    )
    x_halos, grads, carry, activated = [], [], [], []

    def activate(h, preact, *before):
        return call(
            functools.partial(activation_kernel, half, h),
            "activation",
            1.0,
            [((own * (height // 2), half), F32)],
            [pltpu.VMEM((own * (height // 2 // CHUNKS), half), F32), pltpu.SemaphoreType.DMA((own,))],
            preact,
            *before,
            in_place=bool(h),
        )

    for h in range(CHUNKS):
        shapes = [((4 * chans, part_cells), BF16)] * 2 + [((own, part_cells), F32)] * count
        if h < CHUNKS - 1:
            shapes.append(((outs, LANES), F32))
        xh_hi, xh_lo, *pieces = call(
            functools.partial(halo_kernel, dims, own, count, h),
            "halo",
            1.7,
            shapes,
            [pltpu.VMEM((outs, part_cells), F32)],
            halos[h],
            parts[h],
            w_halo,
            *carry,
        )
        x_halos += [xh_hi, xh_lo]
        carry = pieces[count:]
        preact = pieces[0]
        if h:
            preact, activated = lax.optimization_barrier((preact, activated))
        for k in range(1, count):
            preact = preact + turned(pieces[k], "chan", k)
        grad = upstream[:, h * part_cells : (h + 1) * part_cells] * jax.nn.sigmoid(preact)
        if h < CHUNKS - 1:
            activated = list(activate(h, preact, *activated))
        grads.append([grad] + [turned(grad, "chan", k) for k in range(1, count)])
    above = [[from_behind(g, "space", -1) for g in (chunk if h < CHUNKS - 1 else chunk[:1])] for h, chunk in enumerate(grads)]

    summed = []
    for h in range(CHUNKS):
        low = max(h - 1, 0)
        last = h == CHUNKS - 1
        sources = sum(grads[low : h + 1], [])
        if last:
            *early, summed[0] = lax.optimization_barrier((*[chunk[0] for chunk in above], summed[0]))
            for chunk, grad in zip(above, early):
                chunk[0] = grad
            *sent, summed[0] = lax.optimization_barrier((*grads[-1][1:], summed[0]))
            above[-1] += [from_behind(g, "space", -1) for g in sent]
        (result,) = call(
            functools.partial(filter_kernel, dims, own, count, h),
            "filter",
            1.6,
            [((14 * chans, LANES) if last else (12 * chans, 4 * outs), F32)],
            [
                pltpu.VMEM((12 * chans, 4 * outs), F32),
                pltpu.VMEM((outs, (h - low + 1) * part_cells + (LANES if last else 0)), F32),
            ],
            *sources,
            *x_own[2 * low : 2 * h + 2],
            *x_halos[2 * low : 2 * h + 2],
            *summed,
        )
        summed = [result]
    per = height // 4 // CHUNKS
    cuts = [0] + [height // 4 * share // 32 // 2 * 2 for share in BACK] + [height // 4]
    state = {"grad": [], "done": 0}

    def rows_of_grad(value):
        i = state["done"]
        begin, end = cuts[i], cuts[i + 1]
        low, high = begin // per, min(end // per + 1, CHUNKS)
        sources = sum(grads[low:high], []) + sum(above[low:high], [])
        *sources, value = lax.optimization_barrier((*sources, value))
        state["grad"] = call(
            functools.partial(back_kernel, dims, own, count, begin, end, low, high),
            "back",
            2.5,
            [((chans * planes * height, width), F32)],
            [pltpu.VMEM((outs, (high - low) * part_cells + (LANES if high == CHUNKS else 0)), F32)] * 2
            + [pltpu.VMEM((chans * planes * height, width), F32), pltpu.SemaphoreType.DMA((chans * planes,))],
            *sources,
            w_back,
            *state["grad"],
            in_place=bool(i),
        )
        state["done"] += 1
        return value

    def beside(index, value):
        if state["grad"]:
            *state["grad"], value = lax.optimization_barrier((*state["grad"], value))
        if state["done"] == len(cuts) - 2:
            state["preact"], value = lax.optimization_barrier((preact, value))
        return rows_of_grad(value) if state["done"] < len(cuts) - 1 else value

    packed = sum_over(summed[0], "space", beside)
    while state["done"] < len(cuts) - 1:
        packed = rows_of_grad(packed)
    (volume_grad,) = state["grad"]
    (activated,) = activate(CHUNKS - 1, state.get("preact", preact), *activated)
    volume_grad = volume_grad.reshape(chans, planes, height, width)[:real]
    depth_all = planes * lax.axis_size("space")
    factor = float(depth_all // 2 * (height // 2) * half) ** (-0.5)
    unpacked = jnp.concatenate([packed[:, :outs], packed[: 13 * chans, outs:]], axis=0) * factor
    filter_grad = unpacked.reshape(3, 3, 3, chans, outs)[:, :, :, :real].transpose(4, 3, 0, 1, 2)
    return (activated.reshape(cotangent.shape), volume_grad, filter_grad)


def solution(mesh):
    in_specs = (
        P("chan", "space", None, None),
        P(None, "chan", None, None, None),
        P("chan", "space", None, None),
    )
    out_specs = (
        P("chan", "space", None, None),
        P("chan", "space", None, None),
        P(None, "chan", None, None, None),
    )
    return jax.shard_map(
        on_device, mesh=mesh, in_specs=in_specs, out_specs=out_specs, check_vma=False
    )
```

```python
import functools

import jax
import jax.numpy as jnp
from jax import lax
from jax.experimental import pallas as pl
from jax.experimental.pallas import tpu as pltpu
from jax.sharding import PartitionSpec as P

F32 = jnp.float32
BF16 = jnp.bfloat16
LANES = 128
STEP = 8
CHUNKS = 2
BACK = (14,)
VMEM = pl.BlockSpec(memory_space=pltpu.VMEM)
ANY = pl.BlockSpec(memory_space=pl.ANY)

PLACE = {0: (1, 1), 1: (0, 0), 2: (1, 0)}


def split(x):
    hi = x.astype(BF16)
    return hi, (x - hi.astype(F32)).astype(BF16)


def pairing(half, transposed):
    size = 4 * half
    cell = lax.broadcasted_iota(jnp.int32, (size, size), 0 if transposed else 1)
    source = lax.broadcasted_iota(jnp.int32, (size, size), 1 if transposed else 0)
    parity, rest = cell // (2 * half), cell % (2 * half)
    wanted = (rest // half) * (2 * half) + 2 * (rest % half) + parity
    return (source == wanted).astype(F32).astype(BF16)


def lane_of(shape):
    return lax.broadcasted_iota(jnp.int32, shape, 1)


def group(index, count=1):
    return slice(index * LANES, (index + count) * LANES)


def parity_split(load, planes, first, matrix):
    tiles = []
    for plane in range(planes):
        for parity in range(2):
            for j in range(STEP):
                row = 4 * (first + j) + parity
                tiles.append(jnp.concatenate([load(plane, row), load(plane, row + 2)], axis=1))
    chans = tiles[0].shape[0]
    hi, lo = split(jnp.concatenate(tiles, axis=0))
    moved = jnp.dot(jnp.concatenate([hi, lo], axis=0), matrix, preferred_element_type=F32).astype(BF16)
    parts = []
    for part in range(2):
        rows = []
        for parity in range(planes * 2):
            for column in range(2):
                pieces = []
                for j in range(STEP):
                    start = ((part * planes * 2 + parity) * STEP + j) * chans
                    pieces.append(moved[start : start + chans, group(column)])
                rows.append(jnp.concatenate(pieces, axis=1))
        parts.append(jnp.concatenate(rows, axis=0))
    return parts


def shift_add(y, outs, half, carry):
    lane = lane_of((outs, LANES))
    first_column = lane % half == 0
    first_row = lane < half

    def one_column(v):
        return jnp.where(first_column, 0.0, pltpu.roll(v, 1, 1))

    pieces = []
    for j in range(STEP):
        v = [y[s * outs : (s + 1) * outs, group(j)] for s in range(4)]
        here = v[0] + one_column(v[1])
        late = pltpu.roll(v[2] + one_column(v[3]), half, 1)
        pieces.append(here + jnp.where(first_row, carry, late))
        carry = late
    return jnp.concatenate(pieces, axis=1), carry


def grad_shifts(load, first, count, outs, half):
    lane = lane_of((outs, LANES))
    last_column = lane % half == half - 1
    first_row = lane < half

    def one_column(v):
        return jnp.where(last_column, 0.0, pltpu.roll(v, LANES - 1, 1))

    v = [load(first + j) for j in range(count + 1)]
    swapped = [pltpu.roll(a, half, 1) for a in v]
    pieces = []
    for j in range(count):
        later = jnp.where(first_row, swapped[j], swapped[j + 1])
        pieces.append(jnp.concatenate([v[j], one_column(v[j]), later, one_column(later)], axis=0))
    return split(jnp.concatenate(pieces, axis=1))


def gather_grads(pieces, scratch, own, count):
    me = lax.axis_index("chan")
    left = 0
    for chunk in range(len(pieces) // count):
        for k in range(count):
            piece = pieces[chunk * count + k]
            start = pl.multiple_of(lax.rem(me + count - k, count) * own, own)
            scratch[pl.ds(start, own), left : left + piece.shape[1]] = piece[...]
        left += piece.shape[1]
    if left < scratch.shape[1]:
        scratch[:, left:] = jnp.zeros((scratch.shape[0], scratch.shape[1] - left), F32)


def own_kernel(dims, chunk, vol, *refs):
    chans, outs, planes, height, half = dims
    rows = height // CHUNKS
    if chunk:
        w_own, before = refs[:2]
        x_hi, x_lo, part, *rest = refs[2:]
        carry, weights = before[...], w_own[...]
        after = rest[0] if rest else None
    else:
        filt, x_hi, x_lo, part, w_own, w_halo, w_back, after, w_t = refs
        carry, weights = jnp.zeros((outs, LANES), F32), lay_weights(dims, filt, w_t, w_own, w_halo, w_back)
    matrix = pairing(half, False)

    def load(plane, row):
        return vol[pl.ds(plane * height + chunk * rows + row, chans, stride=planes * height), :]

    for first in range(0, rows // 4, STEP):
        hi, lo = parity_split(load, planes, first, matrix)
        cells = group(first, STEP)
        x_hi[:, cells] = hi
        x_lo[:, cells] = lo
        y = jnp.dot(weights, jnp.concatenate([hi, lo, hi], axis=0), preferred_element_type=F32)
        part[:, cells], carry = shift_add(y, outs, half, carry)
    if after is not None:
        after[...] = carry


def lay_weights(dims, filt, w_t, w_own, w_halo, w_back):
    chans, outs, planes, height, half = dims
    w_t[...] = jnp.zeros_like(w_t)
    for p in range(3):
        for q in range(3):
            for r in range(3):
                (rho, sb), (gamma, sc) = PLACE[q], PLACE[r]
                top = ((p * 2 + rho) * 2 + gamma) * chans
                left = (sb * 2 + sc) * outs
                tap = (p * 3 + q) * 3 + r
                w_t[top : top + chans, left : left + outs] = filt[tap * chans : (tap + 1) * chans, :]
    edge = 4 * chans
    hi, lo = split(w_t[...])
    here = jnp.concatenate([hi[edge:], hi[edge:], lo[edge:]], axis=1)
    above = jnp.concatenate([hi[:edge], hi[:edge], lo[:edge]], axis=1)
    w_back[...] = jnp.concatenate([here, jnp.concatenate([jnp.zeros_like(above), above], axis=0)], axis=1)
    hi, lo = hi.astype(F32), lo.astype(F32)
    w_halo[...] = jnp.concatenate([hi[:edge], hi[:edge], lo[:edge]], axis=0).T.astype(BF16)
    hi, lo = split(w_t[edge:, :].T)
    weights = jnp.concatenate([hi, hi, lo], axis=1)
    w_own[...] = weights
    return weights


def halo_kernel(dims, own, count, chunk, *refs):
    chans, outs, planes, height, half = dims
    plane, part, w_halo = refs[:3]
    before = refs[3] if chunk else None
    x_hi, x_lo, *results, total = refs[4 if chunk else 3 :]
    after = results[count] if len(results) > count else None
    matrix = pairing(half, False)
    weights = w_halo[...]
    rows = height // CHUNKS

    def load(_, row):
        return plane[pl.ds(row, chans, stride=rows), :]

    carry = before[...] if chunk else jnp.zeros((outs, LANES), F32)
    for first in range(0, rows // 4, STEP):
        hi, lo = parity_split(load, 1, first, matrix)
        cells = group(first, STEP)
        x_hi[:, cells] = hi
        x_lo[:, cells] = lo
        y = jnp.dot(weights, jnp.concatenate([hi, lo, hi], axis=0), preferred_element_type=F32)
        added, carry = shift_add(y, outs, half, carry)
        total[:, cells] = part[:, cells] + added
    if after is not None:
        after[...] = carry
    me = lax.axis_index("chan")
    for k in range(count):
        start = pl.multiple_of(lax.rem(me + k, count) * own, own)
        results[k][...] = total[pl.ds(start, own), :]


def filter_kernel(dims, own, count, chunk, *refs):
    chans, outs, planes, height, half = dims
    per = height // 4 // CHUNKS
    loaded = min(chunk, 1) + 1
    last = chunk == CHUNKS - 1
    pieces, refs = refs[: loaded * count], refs[loaded * count :]
    planes_x, refs = refs[: 2 * loaded], refs[2 * loaded :]
    halos, refs = refs[: 2 * loaded], refs[2 * loaded :]
    if chunk:
        before, refs = refs[0], refs[1:]
    *out, total, g_all = refs
    gather_grads(pieces, g_all, own, count)
    base = (chunk - loaded + 1) * per
    begin = chunk * per - (1 if chunk else 0)
    end = (chunk + 1) * per - (0 if last else 1)
    total[...] = before[...] if chunk else jnp.zeros_like(total)

    def cells_of(sources, part, first, size):
        found = []
        for h in range(loaded):
            low = max(first - base, h * per)
            high = min(first - base + size, (h + 1) * per)
            if low < high:
                found.append(sources[2 * h + part][:, group(low - h * per, high - low)])
        return found[0] if len(found) == 1 else jnp.concatenate(found, axis=1)

    first = begin
    while first < end:
        size = min(STEP, end - first)
        hi, lo = grad_shifts(lambda g: g_all[:, group(g - base)], first, size, outs, half)
        a_hi, a_lo = [
            jnp.concatenate([cells_of(v, part, first, size) for v in (halos, planes_x)], axis=0) for part in range(2)
        ]
        total[...] += lax.dot_general(
            jnp.concatenate([a_hi, a_hi, a_lo], axis=1),
            jnp.concatenate([hi, lo, hi], axis=1),
            (((1,), (1,)), ((), ())),
            preferred_element_type=F32,
        )
        first += size
    if not last:
        out[0][...] = total[...]
        return
    kept, sent, packed = out

    def tap_block(tap, side):
        p, q, r = tap // 9, tap // 3 % 3, tap % 3
        (rho, sb), (gamma, sc) = PLACE[q], PLACE[r]
        top = ((p * 2 + rho) * 2 + gamma) * chans
        block = total[top : top + chans, group(sb)]
        return block if sc == side else pltpu.roll(block, outs, 1)

    left_side = lane_of((chans, LANES)) < outs
    for tap in range(14):
        right = tap_block(tap + 14, 1) if tap + 14 < 27 else jnp.zeros((chans, LANES), F32)
        packed[tap * chans : (tap + 1) * chans, :] = jnp.where(left_side, tap_block(tap, 0), right)
    size = 7 * chans
    side = lax.rem(lax.axis_index("space"), 2)
    kept[...] = packed[pl.ds(pl.multiple_of(side * size, size), size), :]
    sent[...] = packed[pl.ds(pl.multiple_of((1 - side) * size, size), size), :]


def back_kernel(dims, own, count, begin, end, low, high, *refs):
    chans, outs, planes, height, half = dims
    loaded = high - low
    here, above = refs[: loaded * count], refs[loaded * count : 2 * loaded * count]
    weights = refs[2 * loaded * count][...]
    out, g_here, g_above, grown, sem = refs[-5:]
    gather_grads(here, g_here, own, count)
    gather_grads(above, g_above, own, count)
    base = low * (height // 4 // CHUNKS)
    matrix = pairing(half, True)
    matrix = jnp.concatenate([matrix, matrix], axis=0)
    first = begin
    while first < end:
        size = min(STEP, end - first)
        hi, lo = grad_shifts(lambda g: g_here[:, group(g - base)], first, size, outs, half)
        hi_above, lo_above = grad_shifts(lambda g: g_above[:, group(g - base)], first, size, outs, half)
        grad = jnp.dot(
            weights,
            jnp.concatenate([hi, lo, hi, hi_above, lo_above, hi_above], axis=0),
            preferred_element_type=F32,
        )
        tiles = []
        for parity in range(planes * 2):
            for j in range(size):
                tops = [(parity * 2 + column) * chans for column in range(2)]
                tiles.append(jnp.concatenate([grad[t : t + chans, group(j)] for t in tops], axis=1))
        hi, lo = split(jnp.concatenate(tiles, axis=0))
        rows = jnp.dot(jnp.concatenate([hi, lo], axis=1), matrix, preferred_element_type=F32)
        for parity in range(planes * 2):
            for j in range(size):
                start = (parity * size + j) * chans
                row = (parity // 2) * height + 4 * (first + j) + parity % 2
                for side in range(2):
                    grown[pl.ds(row + 2 * side, chans, stride=planes * height), :] = rows[
                        start : start + chans, group(side)
                    ]
        first += size
    copies = []
    for i in range(chans * planes):
        part = pl.ds(i * height + 4 * begin, 4 * (end - begin))
        copies.append(pltpu.make_async_copy(grown.at[part, :], out.at[part, :], sem.at[i]))
        copies[-1].start()
    for copy in copies:
        copy.wait()


def flat_kernel(half, cube, flat):
    own, cells = flat.shape
    for g in range(cells // LANES):
        sides = [cube[pl.ds(2 * g + side, own, stride=cells // half), :] for side in range(2)]
        flat[:, group(g)] = jnp.concatenate(sides, axis=1)


def activation_kernel(half, h, chunk, *refs):
    out, cube, sem = refs[-3:]
    own, cells = chunk.shape
    rows = cells // half
    for g in range(cells // LANES):
        x = chunk[:, group(g)]
        value = jnp.maximum(x, 0.0) + jnp.log1p(jnp.exp(-jnp.abs(x)))
        cube[pl.ds(2 * g, own, stride=rows), :] = value[:, :half]
        cube[pl.ds(2 * g + 1, own, stride=rows), :] = value[:, half:]
    copies = []
    for i in range(own):
        target = out.at[pl.ds((i * CHUNKS + h) * rows, rows), :]
        copies.append(pltpu.make_async_copy(cube.at[pl.ds(i * rows, rows), :], target, sem.at[i]))
        copies[-1].start()
    for copy in copies:
        copy.wait()


def call(kernel, name, time, shapes, scratch, *args, in_place=False):
    specs = [VMEM] * len(args)
    if in_place:
        specs[-1] = ANY
    return pl.pallas_call(
        kernel,
        name=name,
        out_shape=[jax.ShapeDtypeStruct(s, t) for s, t in shapes],
        in_specs=specs,
        out_specs=[ANY if name in ("back", "activation") else VMEM] * len(shapes),
        scratch_shapes=scratch,
        input_output_aliases={len(args) - 1: 0} if in_place else {},
        cost_estimate=pl.CostEstimate(flops=0, bytes_accessed=int(time * 3.6e2), transcendentals=0),
        compiler_params=pltpu.CompilerParams(vmem_limit_bytes=12 * 1024 * 1024),
    )(*args)


def turned(value, axis, steps):
    count = lax.axis_size(axis)
    return lax.ppermute(value, axis, [(s, (s + steps) % count) for s in range(count)])


def from_behind(value, axis, steps):
    count = lax.axis_size(axis)
    initial, last = (max(0, -steps), min(count, count - steps))
    return lax.ppermute(value, axis, [(source, source + steps) for source in range(initial, last)])


def sum_over(kept, sent, axis, beside):
    count = lax.axis_size(axis)
    assert count > 1 and not count & (count - 1)

    def swapped(value, bit):
        return lax.ppermute(value, axis, [(s, s ^ bit) for s in range(count)])

    value = beside(0, kept + swapped(sent, 1))
    bit = 2
    while bit < count:
        value = beside(bit.bit_length() - 1, value + swapped(value, bit))
        bit *= 2
    other = swapped(value, 1)
    first = lax.rem(lax.axis_index(axis), 2) == 0
    return jnp.where(first, value, other), jnp.where(first, other, value)


def on_device(volume, filters, cotangent):
    real, planes, height, width = volume.shape
    outs = filters.shape[0]
    own = cotangent.shape[0]
    count = lax.axis_size("chan")
    half = width // 2
    cells = (height // 2) * half
    part_cells = cells // CHUNKS
    assert planes == 2 and width == LANES and height % (4 * STEP * CHUNKS) == 0 and 2 * outs == LANES
    chans = -(-real // 16) * 16
    taps = filters.transpose(2, 3, 4, 1, 0)
    if chans > real:
        volume = jnp.pad(volume, ((0, chans - real), (0, 0), (0, 0), (0, 0)))
        taps = jnp.pad(taps, ((0, 0), (0, 0), (0, 0), (0, chans - real), (0, 0)))
    dims = (chans, outs, planes, height, half)
    rows = height // CHUNKS
    halos = [from_behind(volume[:, -1, h * rows : (h + 1) * rows], "space", 1) for h in range(CHUNKS)]
    halos = [halo.reshape(chans * rows, width) for halo in halos]
    x_own, parts, before = [], [], []
    for h in range(CHUNKS):
        shapes = [((8 * chans, part_cells), BF16)] * 2 + [((outs, part_cells), F32)]
        carry = [((outs, LANES), F32)] if h < CHUNKS - 1 else []
        if h:
            results = call(
                functools.partial(own_kernel, dims, h), "own", 1.6, shapes + carry, [], volume.reshape(-1, width), w_own, *before
            )
            before = results[3:]
        else:
            results = call(
                functools.partial(own_kernel, dims, h),
                "own",
                2.2,
                shapes
                + [
                    ((4 * outs, 24 * chans), BF16),
                    ((4 * outs, 12 * chans), BF16),
                    ((8 * chans, 24 * outs), BF16),
                    ((outs, LANES), F32),
                ],
                [pltpu.VMEM((12 * chans, 4 * outs), F32)],
                volume.reshape(-1, width),
                taps.reshape(27 * chans, outs),
            )
            w_own, w_halo, w_back, carried = results[3:]
            before = [carried]
        x_own += results[:2]
        parts.append(results[2])
    (upstream,) = call(
        functools.partial(flat_kernel, half), "flat", 0.8, [((own, cells), F32)], [], cotangent.reshape(-1, half)
    )
    x_halos, grads, above, carry, activated = [], [], [], [], []

    def activate(h, preact, *before):
        return call(
            functools.partial(activation_kernel, half, h),
            "activation",
            1.0,
            [((own * (height // 2), half), F32)],
            [pltpu.VMEM((own * (height // 2 // CHUNKS), half), F32), pltpu.SemaphoreType.DMA((own,))],
            preact,
            *before,
            in_place=bool(h),
        )

    for h in range(CHUNKS):
        shapes = [((4 * chans, part_cells), BF16)] * 2 + [((own, part_cells), F32)] * count
        if h < CHUNKS - 1:
            shapes.append(((outs, LANES), F32))
        xh_hi, xh_lo, *pieces = call(
            functools.partial(halo_kernel, dims, own, count, h),
            "halo",
            1.7,
            shapes,
            [pltpu.VMEM((outs, part_cells), F32)],
            halos[h],
            parts[h],
            w_halo,
            *carry,
        )
        x_halos += [xh_hi, xh_lo]
        carry = pieces[count:]
        preact = pieces[0]
        if h:
            preact, activated = lax.optimization_barrier((preact, activated))
        for k in range(1, count):
            preact = preact + turned(pieces[k], "chan", k)
        grad = upstream[:, h * part_cells : (h + 1) * part_cells] * jax.nn.sigmoid(preact)
        above.append([from_behind(grad, "space", -1)])
        grads.append([grad] + [turned(grad, "chan", k) for k in range(1, count)])
        if h < CHUNKS - 1:
            activated = list(activate(h, preact, *activated))
    for h in range(CHUNKS - 1):
        sent = grads[h][1:]
        above[h] += [from_behind(g, "space", -1) for g in sent]

    summed = []
    for h in range(CHUNKS):
        low = max(h - 1, 0)
        last = h == CHUNKS - 1
        sources = sum(grads[low : h + 1], [])
        if not last:
            sources[0], above[h][0] = lax.optimization_barrier((sources[0], above[h][0]))
        if last:
            *early, summed[0] = lax.optimization_barrier((*[chunk[0] for chunk in above], summed[0]))
            for chunk, grad in zip(above, early):
                chunk[0] = grad
            *sent, summed[0] = lax.optimization_barrier((*grads[-1][1:], summed[0]))
            above[-1] += [from_behind(g, "space", -1) for g in sent]
        summed = call(
            functools.partial(filter_kernel, dims, own, count, h),
            "filter",
            1.6,
            [((7 * chans, LANES), F32)] * 2 if last else [((12 * chans, 4 * outs), F32)],
            ([pltpu.VMEM((14 * chans, LANES), F32)] if last else [])
            + [
                pltpu.VMEM((12 * chans, 4 * outs), F32),
                pltpu.VMEM((outs, (h - low + 1) * part_cells + (LANES if last else 0)), F32),
            ],
            *sources,
            *x_own[2 * low : 2 * h + 2],
            *x_halos[2 * low : 2 * h + 2],
            *summed,
        )
        summed = list(summed)
    per = height // 4 // CHUNKS
    cuts = [0] + [height // 4 * share // 32 // 2 * 2 for share in BACK] + [height // 4]
    state = {"grad": [], "done": 0}

    def rows_of_grad(value):
        i = state["done"]
        begin, end = cuts[i], cuts[i + 1]
        low, high = begin // per, min(end // per + 1, CHUNKS)
        sources = sum(grads[low:high], []) + sum(above[low:high], [])
        *sources, value = lax.optimization_barrier((*sources, value))
        state["grad"] = call(
            functools.partial(back_kernel, dims, own, count, begin, end, low, high),
            "back",
            2.5,
            [((chans * planes * height, width), F32)],
            [pltpu.VMEM((outs, (high - low) * part_cells + (LANES if high == CHUNKS else 0)), F32)] * 2
            + [pltpu.VMEM((chans * planes * height, width), F32), pltpu.SemaphoreType.DMA((chans * planes,))],
            *sources,
            w_back,
            *state["grad"],
            in_place=bool(i),
        )
        state["done"] += 1
        return value

    def beside(index, value):
        for started in ("grad", "activated"):
            if state.get(started):
                *state[started], value = lax.optimization_barrier((*state[started], value))
        if state["done"] < len(cuts) - 1:
            return rows_of_grad(value)
        if "activated" not in state:
            shown, value = lax.optimization_barrier((preact, value))
            state["activated"] = list(activate(CHUNKS - 1, shown, *activated))
        return value

    low, high = sum_over(*summed, "space", beside)
    while state["done"] < len(cuts) - 1:
        low = rows_of_grad(low)
    (volume_grad,) = state["grad"]
    (activated,) = state.get("activated") or activate(CHUNKS - 1, preact, *activated)
    volume_grad = volume_grad.reshape(chans, planes, height, width)[:real]
    depth_all = planes * lax.axis_size("space")
    factor = float(depth_all // 2 * (height // 2) * half) ** (-0.5)
    unpacked = jnp.concatenate([low[:, :outs], high[:, :outs], low[:, outs:], high[:-chans, outs:]], axis=0) * factor
    filter_grad = unpacked.reshape(3, 3, 3, chans, outs)[:, :, :, :real].transpose(4, 3, 0, 1, 2)
    return (activated.reshape(cotangent.shape), volume_grad, filter_grad)


def solution(mesh):
    in_specs = (
        P("chan", "space", None, None),
        P(None, "chan", None, None, None),
        P("chan", "space", None, None),
    )
    out_specs = (
        P("chan", "space", None, None),
        P("chan", "space", None, None),
        P(None, "chan", None, None, None),
    )
    return jax.shard_map(
        on_device, mesh=mesh, in_specs=in_specs, out_specs=out_specs, check_vma=False
    )
```

```python
import functools

import jax
import jax.numpy as jnp
from jax import lax
from jax.experimental import pallas as pl
from jax.experimental.pallas import tpu as pltpu
from jax.sharding import PartitionSpec as P

F32 = jnp.float32
BF16 = jnp.bfloat16
LANES = 128
STEP = 8
CHUNKS = 2
BACK = (8, 22)
VMEM = pl.BlockSpec(memory_space=pltpu.VMEM)
ANY = pl.BlockSpec(memory_space=pl.ANY)

PLACE = {0: (1, 1), 1: (0, 0), 2: (1, 0)}


def split(x):
    hi = x.astype(BF16)
    return hi, (x - hi.astype(F32)).astype(BF16)


def pairing(half, transposed):
    size = 4 * half
    cell = lax.broadcasted_iota(jnp.int32, (size, size), 0 if transposed else 1)
    source = lax.broadcasted_iota(jnp.int32, (size, size), 1 if transposed else 0)
    parity, rest = cell // (2 * half), cell % (2 * half)
    wanted = (rest // half) * (2 * half) + 2 * (rest % half) + parity
    return (source == wanted).astype(F32).astype(BF16)


def lane_of(shape):
    return lax.broadcasted_iota(jnp.int32, shape, 1)


def group(index, count=1):
    return slice(index * LANES, (index + count) * LANES)


def parity_split(load, planes, first, matrix):
    tiles = []
    for plane in range(planes):
        for parity in range(2):
            for j in range(STEP):
                row = 4 * (first + j) + parity
                tiles.append(jnp.concatenate([load(plane, row), load(plane, row + 2)], axis=1))
    chans = tiles[0].shape[0]
    hi, lo = split(jnp.concatenate(tiles, axis=0))
    moved = jnp.dot(jnp.concatenate([hi, lo], axis=0), matrix, preferred_element_type=F32).astype(BF16)
    parts = []
    for part in range(2):
        rows = []
        for parity in range(planes * 2):
            for column in range(2):
                pieces = []
                for j in range(STEP):
                    start = ((part * planes * 2 + parity) * STEP + j) * chans
                    pieces.append(moved[start : start + chans, group(column)])
                rows.append(jnp.concatenate(pieces, axis=1))
        parts.append(jnp.concatenate(rows, axis=0))
    return parts


def shift_add(y, outs, half, carry):
    lane = lane_of((outs, LANES))
    first_column = lane % half == 0
    first_row = lane < half

    def one_column(v):
        return jnp.where(first_column, 0.0, pltpu.roll(v, 1, 1))

    pieces = []
    for j in range(STEP):
        v = [y[s * outs : (s + 1) * outs, group(j)] for s in range(4)]
        here = v[0] + one_column(v[1])
        late = pltpu.roll(v[2] + one_column(v[3]), half, 1)
        pieces.append(here + jnp.where(first_row, carry, late))
        carry = late
    return jnp.concatenate(pieces, axis=1), carry


def grad_shifts(load, first, count, outs, half):
    lane = lane_of((outs, LANES))
    last_column = lane % half == half - 1
    first_row = lane < half

    def one_column(v):
        return jnp.where(last_column, 0.0, pltpu.roll(v, LANES - 1, 1))

    v = [load(first + j) for j in range(count + 1)]
    swapped = [pltpu.roll(a, half, 1) for a in v]
    pieces = []
    for j in range(count):
        later = jnp.where(first_row, swapped[j], swapped[j + 1])
        pieces.append(jnp.concatenate([v[j], one_column(v[j]), later, one_column(later)], axis=0))
    return split(jnp.concatenate(pieces, axis=1))


def gather_grads(pieces, scratch, own, count, begin, end):
    me = lax.axis_index("chan")
    per = pieces[0].shape[1] // LANES
    chunks = len(pieces) // count
    for chunk in range(chunks):
        low, high = max(begin, chunk * per), min(end, (chunk + 1) * per)
        for k in range(count):
            start = pl.multiple_of(lax.rem(me + count - k, count) * own, own)
            piece = pieces[chunk * count + k]
            scratch[pl.ds(start, own), group(low - begin, high - low)] = piece[:, group(low - chunk * per, high - low)]
    if end > chunks * per:
        scratch[:, group(chunks * per - begin)] = jnp.zeros((scratch.shape[0], LANES), F32)


def own_kernel(dims, chunk, vol, *refs):
    chans, outs, planes, height, half = dims
    rows = height // CHUNKS
    if chunk:
        w_own, before = refs[:2]
        x_hi, x_lo, part, *rest = refs[2:]
        carry, weights = before[...], w_own[...]
        after = rest[0] if rest else None
    else:
        filt, x_hi, x_lo, part, w_own, w_halo, w_back, after, w_t = refs
        carry, weights = jnp.zeros((outs, LANES), F32), lay_weights(dims, filt, w_t, w_own, w_halo, w_back)
    matrix = pairing(half, False)

    def load(plane, row):
        return vol[pl.ds(plane * height + chunk * rows + row, chans, stride=planes * height), :]

    for first in range(0, rows // 4, STEP):
        hi, lo = parity_split(load, planes, first, matrix)
        cells = group(first, STEP)
        x_hi[:, cells] = hi
        x_lo[:, cells] = lo
        y = jnp.dot(weights, jnp.concatenate([hi, lo, hi], axis=0), preferred_element_type=F32)
        part[:, cells], carry = shift_add(y, outs, half, carry)
    if after is not None:
        after[...] = carry


def lay_weights(dims, filt, w_t, w_own, w_halo, w_back):
    chans, outs, planes, height, half = dims
    w_t[...] = jnp.zeros_like(w_t)
    for p in range(3):
        for q in range(3):
            for r in range(3):
                (rho, sb), (gamma, sc) = PLACE[q], PLACE[r]
                top = ((p * 2 + rho) * 2 + gamma) * chans
                left = (sb * 2 + sc) * outs
                tap = (p * 3 + q) * 3 + r
                w_t[top : top + chans, left : left + outs] = filt[tap * chans : (tap + 1) * chans, :]
    edge = 4 * chans
    hi, lo = split(w_t[...])
    here = jnp.concatenate([hi[edge:], hi[edge:], lo[edge:]], axis=1)
    above = jnp.concatenate([hi[:edge], hi[:edge], lo[:edge]], axis=1)
    w_back[...] = jnp.concatenate([here, jnp.concatenate([jnp.zeros_like(above), above], axis=0)], axis=1)
    hi, lo = hi.astype(F32), lo.astype(F32)
    w_halo[...] = jnp.concatenate([hi[:edge], hi[:edge], lo[:edge]], axis=0).T.astype(BF16)
    hi, lo = split(w_t[edge:, :].T)
    weights = jnp.concatenate([hi, hi, lo], axis=1)
    w_own[...] = weights
    return weights


def halo_kernel(dims, own, count, chunk, *refs):
    chans, outs, planes, height, half = dims
    plane, part, w_halo = refs[:3]
    before = refs[3] if chunk else None
    x_hi, x_lo, *results, total = refs[4 if chunk else 3 :]
    after = results[count] if len(results) > count else None
    matrix = pairing(half, False)
    weights = w_halo[...]
    rows = height // CHUNKS

    def load(_, row):
        return plane[pl.ds(row, chans, stride=rows), :]

    carry = before[...] if chunk else jnp.zeros((outs, LANES), F32)
    for first in range(0, rows // 4, STEP):
        hi, lo = parity_split(load, 1, first, matrix)
        cells = group(first, STEP)
        x_hi[:, cells] = hi
        x_lo[:, cells] = lo
        y = jnp.dot(weights, jnp.concatenate([hi, lo, hi], axis=0), preferred_element_type=F32)
        added, carry = shift_add(y, outs, half, carry)
        total[:, cells] = part[:, cells] + added
    if after is not None:
        after[...] = carry
    me = lax.axis_index("chan")
    for k in range(count):
        start = pl.multiple_of(lax.rem(me + k, count) * own, own)
        results[k][...] = total[pl.ds(start, own), :]


def filter_kernel(dims, own, count, chunk, *refs):
    chans, outs, planes, height, half = dims
    per = height // 4 // CHUNKS
    loaded = min(chunk, 1) + 1
    last = chunk == CHUNKS - 1
    pieces, refs = refs[: loaded * count], refs[loaded * count :]
    planes_x, refs = refs[: 2 * loaded], refs[2 * loaded :]
    halos, refs = refs[: 2 * loaded], refs[2 * loaded :]
    if chunk:
        before, refs = refs[0], refs[1:]
    *out, total, g_all = refs
    base = (chunk - loaded + 1) * per
    begin = chunk * per - (1 if chunk else 0)
    end = (chunk + 1) * per - (0 if last else 1)
    gather_grads(pieces, g_all, own, count, begin - base, end + 1 - base)
    total[...] = before[...] if chunk else jnp.zeros_like(total)

    def cells_of(sources, part, first, size):
        found = []
        for h in range(loaded):
            low = max(first - base, h * per)
            high = min(first - base + size, (h + 1) * per)
            if low < high:
                found.append(sources[2 * h + part][:, group(low - h * per, high - low)])
        return found[0] if len(found) == 1 else jnp.concatenate(found, axis=1)

    first = begin
    while first < end:
        size = min(STEP, end - first)
        hi, lo = grad_shifts(lambda g: g_all[:, group(g - begin)], first, size, outs, half)
        a_hi, a_lo = [
            jnp.concatenate([cells_of(v, part, first, size) for v in (halos, planes_x)], axis=0) for part in range(2)
        ]
        total[...] += lax.dot_general(
            jnp.concatenate([a_hi, a_hi, a_lo], axis=1),
            jnp.concatenate([hi, lo, hi], axis=1),
            (((1,), (1,)), ((), ())),
            preferred_element_type=F32,
        )
        first += size
    if not last:
        out[0][...] = total[...]
        return
    kept, sent, packed = out

    def tap_block(tap, side):
        p, q, r = tap // 9, tap // 3 % 3, tap % 3
        (rho, sb), (gamma, sc) = PLACE[q], PLACE[r]
        top = ((p * 2 + rho) * 2 + gamma) * chans
        block = total[top : top + chans, group(sb)]
        return block if sc == side else pltpu.roll(block, outs, 1)

    left_side = lane_of((chans, LANES)) < outs
    for tap in range(14):
        right = tap_block(tap + 14, 1) if tap + 14 < 27 else jnp.zeros((chans, LANES), F32)
        packed[tap * chans : (tap + 1) * chans, :] = jnp.where(left_side, tap_block(tap, 0), right)
    size = 7 * chans
    side = lax.rem(lax.axis_index("space"), 2)
    kept[...] = packed[pl.ds(pl.multiple_of(side * size, size), size), :]
    sent[...] = packed[pl.ds(pl.multiple_of((1 - side) * size, size), size), :]


def back_kernel(dims, own, count, begin, end, low, high, *refs):
    chans, outs, planes, height, half = dims
    loaded = high - low
    here, above = refs[: loaded * count], refs[loaded * count : 2 * loaded * count]
    weights = refs[2 * loaded * count][...]
    out, g_here, g_above, grown, sem = refs[-5:]
    base = low * (height // 4 // CHUNKS)
    gather_grads(here, g_here, own, count, begin - base, end + 1 - base)
    gather_grads(above, g_above, own, count, begin - base, end + 1 - base)
    flat = grown.reshape(chans * planes * height, LANES)
    matrix = pairing(half, True)
    matrix = jnp.concatenate([matrix, matrix], axis=0)
    first = begin
    while first < end:
        size = min(STEP, end - first)
        hi, lo = grad_shifts(lambda g: g_here[:, group(g - begin)], first, size, outs, half)
        hi_above, lo_above = grad_shifts(lambda g: g_above[:, group(g - begin)], first, size, outs, half)
        grad = jnp.dot(
            weights,
            jnp.concatenate([hi, lo, hi, hi_above, lo_above, hi_above], axis=0),
            preferred_element_type=F32,
        )
        tiles = []
        for parity in range(planes * 2):
            for j in range(size):
                tops = [(parity * 2 + column) * chans for column in range(2)]
                tiles.append(jnp.concatenate([grad[t : t + chans, group(j)] for t in tops], axis=1))
        hi, lo = split(jnp.concatenate(tiles, axis=0))
        rows = jnp.dot(jnp.concatenate([hi, lo], axis=1), matrix, preferred_element_type=F32)
        for parity in range(planes * 2):
            for j in range(size):
                start = (parity * size + j) * chans
                row = (parity // 2) * height + 4 * (first + j) + parity % 2
                for side in range(2):
                    flat[pl.ds(row + 2 * side, chans, stride=planes * height), :] = rows[
                        start : start + chans, group(side)
                    ]
        first += size
    part = pl.ds(4 * begin, 4 * (end - begin))
    copy = pltpu.make_async_copy(grown.at[:, part, :], out.at[:, part, :], sem)
    copy.start()
    copy.wait()


def flat_kernel(half, cube, flat):
    own, cells = flat.shape
    for g in range(cells // LANES):
        sides = [cube[pl.ds(2 * g + side, own, stride=cells // half), :] for side in range(2)]
        flat[:, group(g)] = jnp.concatenate(sides, axis=1)


def activation_kernel(half, h, chunk, *refs):
    out, cube, sem = refs[-3:]
    own, cells = chunk.shape
    rows = cells // half
    for g in range(cells // LANES):
        x = chunk[:, group(g)]
        value = jnp.maximum(x, 0.0) + jnp.log1p(jnp.exp(-jnp.abs(x)))
        cube[pl.ds(2 * g, own, stride=rows), :] = value[:, :half]
        cube[pl.ds(2 * g + 1, own, stride=rows), :] = value[:, half:]
    copies = []
    for i in range(own):
        target = out.at[pl.ds((i * CHUNKS + h) * rows, rows), :]
        copies.append(pltpu.make_async_copy(cube.at[pl.ds(i * rows, rows), :], target, sem.at[i]))
        copies[-1].start()
    for copy in copies:
        copy.wait()


def call(kernel, name, time, shapes, scratch, *args, in_place=False):
    specs = [VMEM] * len(args)
    if in_place:
        specs[-1] = ANY
    return pl.pallas_call(
        kernel,
        name=name,
        out_shape=[jax.ShapeDtypeStruct(s, t) for s, t in shapes],
        in_specs=specs,
        out_specs=[ANY if name in ("back", "activation") else VMEM] * len(shapes),
        scratch_shapes=scratch,
        input_output_aliases={len(args) - 1: 0} if in_place else {},
        cost_estimate=pl.CostEstimate(flops=0, bytes_accessed=int(time * 3.6e2), transcendentals=0),
        compiler_params=pltpu.CompilerParams(vmem_limit_bytes=12 * 1024 * 1024),
    )(*args)


def turned(value, axis, steps):
    count = lax.axis_size(axis)
    return lax.ppermute(value, axis, [(s, (s + steps) % count) for s in range(count)])


def from_behind(value, axis, steps):
    count = lax.axis_size(axis)
    initial, last = (max(0, -steps), min(count, count - steps))
    return lax.ppermute(value, axis, [(source, source + steps) for source in range(initial, last)])


def sum_over(kept, sent, axis, beside):
    count = lax.axis_size(axis)
    assert count > 1 and not count & (count - 1)

    def swapped(value, bit):
        return lax.ppermute(value, axis, [(s, s ^ bit) for s in range(count)])

    value = beside(0, kept + swapped(sent, 1))
    bit = 2
    while bit < count:
        value = beside(bit.bit_length() - 1, value + swapped(value, bit))
        bit *= 2
    other = swapped(value, 1)
    first = lax.rem(lax.axis_index(axis), 2) == 0
    return jnp.where(first, value, other), jnp.where(first, other, value)


def on_device(volume, filters, cotangent):
    real, planes, height, width = volume.shape
    outs = filters.shape[0]
    own = cotangent.shape[0]
    count = lax.axis_size("chan")
    half = width // 2
    cells = (height // 2) * half
    part_cells = cells // CHUNKS
    assert planes == 2 and width == LANES and height % (4 * STEP * CHUNKS) == 0 and 2 * outs == LANES
    chans = -(-real // 16) * 16
    taps = filters.transpose(2, 3, 4, 1, 0)
    if chans > real:
        volume = jnp.pad(volume, ((0, chans - real), (0, 0), (0, 0), (0, 0)))
        taps = jnp.pad(taps, ((0, 0), (0, 0), (0, 0), (0, chans - real), (0, 0)))
    dims = (chans, outs, planes, height, half)
    rows = height // CHUNKS
    halos = [from_behind(volume[:, -1, h * rows : (h + 1) * rows], "space", 1) for h in range(CHUNKS)]
    halos = [halo.reshape(chans * rows, width) for halo in halos]
    x_own, parts, before = [], [], []
    for h in range(CHUNKS):
        shapes = [((8 * chans, part_cells), BF16)] * 2 + [((outs, part_cells), F32)]
        carry = [((outs, LANES), F32)] if h < CHUNKS - 1 else []
        if h:
            results = call(
                functools.partial(own_kernel, dims, h), "own", 1.6, shapes + carry, [], volume.reshape(-1, width), w_own, *before
            )
            before = results[3:]
        else:
            results = call(
                functools.partial(own_kernel, dims, h),
                "own",
                2.2,
                shapes
                + [
                    ((4 * outs, 24 * chans), BF16),
                    ((4 * outs, 12 * chans), BF16),
                    ((8 * chans, 24 * outs), BF16),
                    ((outs, LANES), F32),
                ],
                [pltpu.VMEM((12 * chans, 4 * outs), F32)],
                volume.reshape(-1, width),
                taps.reshape(27 * chans, outs),
            )
            w_own, w_halo, w_back, carried = results[3:]
            before = [carried]
        x_own += results[:2]
        parts.append(results[2])
    (upstream,) = call(
        functools.partial(flat_kernel, half), "flat", 0.8, [((own, cells), F32)], [], cotangent.reshape(-1, half)
    )
    x_halos, grads, above, carry, activated = [], [], [], [], []

    def activate(h, preact, *before):
        return call(
            functools.partial(activation_kernel, half, h),
            "activation",
            1.0,
            [((own * (height // 2), half), F32)],
            [pltpu.VMEM((own * (height // 2 // CHUNKS), half), F32), pltpu.SemaphoreType.DMA((own,))],
            preact,
            *before,
            in_place=bool(h),
        )

    for h in range(CHUNKS):
        shapes = [((4 * chans, part_cells), BF16)] * 2 + [((own, part_cells), F32)] * count
        if h < CHUNKS - 1:
            shapes.append(((outs, LANES), F32))
        xh_hi, xh_lo, *pieces = call(
            functools.partial(halo_kernel, dims, own, count, h),
            "halo",
            1.7,
            shapes,
            [pltpu.VMEM((outs, part_cells), F32)],
            halos[h],
            parts[h],
            w_halo,
            *carry,
        )
        x_halos += [xh_hi, xh_lo]
        carry = pieces[count:]
        preact = pieces[0]
        if h:
            preact, activated = lax.optimization_barrier((preact, activated))
        for k in range(1, count):
            preact = preact + turned(pieces[k], "chan", k)
        grad = upstream[:, h * part_cells : (h + 1) * part_cells] * jax.nn.sigmoid(preact)
        above.append([from_behind(grad, "space", -1)])
        grads.append([grad] + [turned(grad, "chan", k) for k in range(1, count)])
        if h < CHUNKS - 1:
            activated = list(activate(h, preact, *activated))
    for h in range(CHUNKS - 1):
        sent = grads[h][1:]
        above[h] += [from_behind(g, "space", -1) for g in sent]

    summed = []
    for h in range(CHUNKS):
        low = max(h - 1, 0)
        last = h == CHUNKS - 1
        sources = sum(grads[low : h + 1], [])
        if not last:
            sources[0], above[h][0] = lax.optimization_barrier((sources[0], above[h][0]))
        if last:
            *early, summed[0] = lax.optimization_barrier((*[chunk[0] for chunk in above], summed[0]))
            for chunk, grad in zip(above, early):
                chunk[0] = grad
            shown, summed[0] = lax.optimization_barrier((preact, summed[0]))
            activated = list(activate(CHUNKS - 1, shown, *activated))
            *sent, summed[0], activated[0] = lax.optimization_barrier((*grads[-1][1:], summed[0], activated[0]))
            above[-1] += [from_behind(g, "space", -1) for g in sent]
        summed = call(
            functools.partial(filter_kernel, dims, own, count, h),
            "filter",
            1.6,
            [((7 * chans, LANES), F32)] * 2 if last else [((12 * chans, 4 * outs), F32)],
            ([pltpu.VMEM((14 * chans, LANES), F32)] if last else [])
            + [
                pltpu.VMEM((12 * chans, 4 * outs), F32),
                pltpu.VMEM((outs, part_cells + (LANES * (2 if last else 1) if h else 0)), F32),
            ],
            *sources,
            *x_own[2 * low : 2 * h + 2],
            *x_halos[2 * low : 2 * h + 2],
            *summed,
        )
        summed = list(summed)
    per = height // 4 // CHUNKS
    cuts = [0] + [height // 4 * share // 32 // 2 * 2 for share in BACK] + [height // 4]
    state = {"grad": [], "done": 0}

    def rows_of_grad(value):
        i = state["done"]
        begin, end = cuts[i], cuts[i + 1]
        low, high = begin // per, min(end // per + 1, CHUNKS)
        sources = sum(grads[low:high], []) + sum(above[low:high], [])
        *sources, value = lax.optimization_barrier((*sources, value))
        state["grad"] = call(
            functools.partial(back_kernel, dims, own, count, begin, end, low, high),
            "back",
            2.5,
            [((chans * planes, height, width), F32)],
            [pltpu.VMEM((outs, (end + 1 - begin) * LANES), F32)] * 2
            + [pltpu.VMEM((chans * planes, height, width), F32), pltpu.SemaphoreType.DMA],
            *sources,
            w_back,
            *state["grad"],
            in_place=bool(i),
        )
        state["done"] += 1
        return value

    def beside(index, value):
        if state["grad"]:
            *state["grad"], value = lax.optimization_barrier((*state["grad"], value))
        return rows_of_grad(value) if state["done"] < len(cuts) - 1 else value

    low, high = sum_over(*summed, "space", beside)
    while state["done"] < len(cuts) - 1:
        low = rows_of_grad(low)
    (volume_grad,) = state["grad"]
    (activated,) = activated
    volume_grad = volume_grad.reshape(chans, planes, height, width)[:real]
    depth_all = planes * lax.axis_size("space")
    factor = float(depth_all // 2 * (height // 2) * half) ** (-0.5)
    unpacked = jnp.concatenate([low[:, :outs], high[:, :outs], low[:, outs:], high[:-chans, outs:]], axis=0) * factor
    filter_grad = unpacked.reshape(3, 3, 3, chans, outs)[:, :, :, :real].transpose(4, 3, 0, 1, 2)
    return (activated.reshape(cotangent.shape), volume_grad, filter_grad)


def solution(mesh):
    in_specs = (
        P("chan", "space", None, None),
        P(None, "chan", None, None, None),
        P("chan", "space", None, None),
    )
    out_specs = (
        P("chan", "space", None, None),
        P("chan", "space", None, None),
        P(None, "chan", None, None, None),
    )
    return jax.shard_map(
        on_device, mesh=mesh, in_specs=in_specs, out_specs=out_specs, check_vma=False
    )
```

```python
import functools

import jax
import jax.numpy as jnp
from jax import lax
from jax.experimental import pallas as pl
from jax.experimental.pallas import tpu as pltpu
from jax.sharding import PartitionSpec as P

F32 = jnp.float32
BF16 = jnp.bfloat16
LANES = 128
STEP = 8
CHUNKS = 2
BACK = (10, 22)
VMEM = pl.BlockSpec(memory_space=pltpu.VMEM)
ANY = pl.BlockSpec(memory_space=pl.ANY)

PLACE = {0: (1, 1), 1: (0, 0), 2: (1, 0)}


def split(x):
    hi = x.astype(BF16)
    return hi, (x - hi.astype(F32)).astype(BF16)


def pairing(half, transposed):
    size = 4 * half
    cell = lax.broadcasted_iota(jnp.int32, (size, size), 0 if transposed else 1)
    source = lax.broadcasted_iota(jnp.int32, (size, size), 1 if transposed else 0)
    parity, rest = cell // (2 * half), cell % (2 * half)
    wanted = (rest // half) * (2 * half) + 2 * (rest % half) + parity
    return (source == wanted).astype(F32).astype(BF16)


def steps(begin, end):
    runs = -(-(end - begin) // (STEP + 1))
    cuts = [begin + (end - begin) * i // runs for i in range(runs + 1)]
    return [(low, high - low) for low, high in zip(cuts, cuts[1:])]


def lane_of(shape):
    return lax.broadcasted_iota(jnp.int32, shape, 1)


def group(index, count=1):
    return slice(index * LANES, (index + count) * LANES)


def parity_split(load, planes, first, matrix):
    tiles = []
    for plane in range(planes):
        for parity in range(2):
            for j in range(STEP):
                row = 4 * (first + j) + parity
                tiles.append(jnp.concatenate([load(plane, row), load(plane, row + 2)], axis=1))
    chans = tiles[0].shape[0]
    hi, lo = split(jnp.concatenate(tiles, axis=0))
    moved = jnp.dot(jnp.concatenate([hi, lo], axis=0), matrix, preferred_element_type=F32).astype(BF16)
    parts = []
    for part in range(2):
        rows = []
        for parity in range(planes * 2):
            for column in range(2):
                pieces = []
                for j in range(STEP):
                    start = ((part * planes * 2 + parity) * STEP + j) * chans
                    pieces.append(moved[start : start + chans, group(column)])
                rows.append(jnp.concatenate(pieces, axis=1))
        parts.append(jnp.concatenate(rows, axis=0))
    return parts


def shift_add(y, outs, half, carry):
    lane = lane_of((outs, LANES))
    first_column = lane % half == 0
    first_row = lane < half

    def one_column(v):
        return jnp.where(first_column, 0.0, pltpu.roll(v, 1, 1))

    pieces = []
    for j in range(STEP):
        v = [y[s * outs : (s + 1) * outs, group(j)] for s in range(4)]
        here = v[0] + one_column(v[1])
        late = pltpu.roll(v[2] + one_column(v[3]), half, 1)
        pieces.append(here + jnp.where(first_row, carry, late))
        carry = late
    return jnp.concatenate(pieces, axis=1), carry


def grad_shifts(load, first, count, outs, half):
    lane = lane_of((outs, LANES))
    last_column = lane % half == half - 1
    first_row = lane < half

    def one_column(v):
        return jnp.where(last_column, 0.0, pltpu.roll(v, LANES - 1, 1))

    v = [load(first + j) for j in range(count + 1)]
    swapped = [pltpu.roll(a, half, 1) for a in v]
    pieces = []
    for j in range(count):
        later = jnp.where(first_row, swapped[j], swapped[j + 1])
        pieces.append(jnp.concatenate([v[j], one_column(v[j]), later, one_column(later)], axis=0))
    return split(jnp.concatenate(pieces, axis=1))


def gather_grads(pieces, scratch, own, count, begin, end):
    me = lax.axis_index("chan")
    per = pieces[0].shape[1] // LANES
    chunks = len(pieces) // count
    for chunk in range(chunks):
        low, high = max(begin, chunk * per), min(end, (chunk + 1) * per)
        for k in range(count):
            start = pl.multiple_of(lax.rem(me + count - k, count) * own, own)
            piece = pieces[chunk * count + k]
            scratch[pl.ds(start, own), group(low - begin, high - low)] = piece[:, group(low - chunk * per, high - low)]
    if end > chunks * per:
        scratch[:, group(chunks * per - begin)] = jnp.zeros((scratch.shape[0], LANES), F32)


def own_kernel(dims, chunk, vol, *refs):
    chans, outs, planes, height, half = dims
    rows = height // CHUNKS
    if chunk:
        w_own, before = refs[:2]
        x_hi, x_lo, part, *rest = refs[2:]
        carry, weights = before[...], w_own[...]
        after = rest[0] if rest else None
    else:
        filt, x_hi, x_lo, part, w_own, w_halo, w_back, after, w_t = refs
        carry, weights = jnp.zeros((outs, LANES), F32), lay_weights(dims, filt, w_t, w_own, w_halo, w_back)
    matrix = pairing(half, False)

    def load(plane, row):
        return vol[pl.ds(plane * height + chunk * rows + row, chans, stride=planes * height), :]

    for first in range(0, rows // 4, STEP):
        hi, lo = parity_split(load, planes, first, matrix)
        cells = group(first, STEP)
        x_hi[:, cells] = hi
        x_lo[:, cells] = lo
        y = jnp.dot(weights, jnp.concatenate([hi, lo, hi], axis=0), preferred_element_type=F32)
        part[:, cells], carry = shift_add(y, outs, half, carry)
    if after is not None:
        after[...] = carry


def lay_weights(dims, filt, w_t, w_own, w_halo, w_back):
    chans, outs, planes, height, half = dims
    w_t[...] = jnp.zeros_like(w_t)
    for p in range(3):
        for q in range(3):
            for r in range(3):
                (rho, sb), (gamma, sc) = PLACE[q], PLACE[r]
                top = ((p * 2 + rho) * 2 + gamma) * chans
                left = (sb * 2 + sc) * outs
                tap = (p * 3 + q) * 3 + r
                w_t[top : top + chans, left : left + outs] = filt[tap * chans : (tap + 1) * chans, :]
    edge = 4 * chans
    hi, lo = split(w_t[...])
    here = jnp.concatenate([hi[edge:], hi[edge:], lo[edge:]], axis=1)
    above = jnp.concatenate([hi[:edge], hi[:edge], lo[:edge]], axis=1)
    w_back[...] = jnp.concatenate([here, jnp.concatenate([jnp.zeros_like(above), above], axis=0)], axis=1)
    hi, lo = hi.astype(F32), lo.astype(F32)
    w_halo[...] = jnp.concatenate([hi[:edge], hi[:edge], lo[:edge]], axis=0).T.astype(BF16)
    hi, lo = split(w_t[edge:, :].T)
    weights = jnp.concatenate([hi, hi, lo], axis=1)
    w_own[...] = weights
    return weights


def halo_kernel(dims, own, count, chunk, *refs):
    chans, outs, planes, height, half = dims
    plane, part, w_halo = refs[:3]
    before = refs[3] if chunk else None
    x_hi, x_lo, *results, total = refs[4 if chunk else 3 :]
    after = results[count] if len(results) > count else None
    matrix = pairing(half, False)
    weights = w_halo[...]
    rows = height // CHUNKS

    def load(_, row):
        return plane[pl.ds(row, chans, stride=rows), :]

    carry = before[...] if chunk else jnp.zeros((outs, LANES), F32)
    for first in range(0, rows // 4, STEP):
        hi, lo = parity_split(load, 1, first, matrix)
        cells = group(first, STEP)
        x_hi[:, cells] = hi
        x_lo[:, cells] = lo
        y = jnp.dot(weights, jnp.concatenate([hi, lo, hi], axis=0), preferred_element_type=F32)
        added, carry = shift_add(y, outs, half, carry)
        total[:, cells] = part[:, cells] + added
    if after is not None:
        after[...] = carry
    me = lax.axis_index("chan")
    for k in range(count):
        start = pl.multiple_of(lax.rem(me + k, count) * own, own)
        results[k][...] = total[pl.ds(start, own), :]


def filter_kernel(dims, own, count, chunk, *refs):
    chans, outs, planes, height, half = dims
    per = height // 4 // CHUNKS
    loaded = min(chunk, 1) + 1
    last = chunk == CHUNKS - 1
    pieces, refs = refs[: loaded * count], refs[loaded * count :]
    planes_x, refs = refs[: 2 * loaded], refs[2 * loaded :]
    halos, refs = refs[: 2 * loaded], refs[2 * loaded :]
    if chunk:
        before, refs = refs[0], refs[1:]
    *out, total, g_all = refs
    base = (chunk - loaded + 1) * per
    begin = chunk * per - (1 if chunk else 0)
    end = (chunk + 1) * per - (0 if last else 1)
    gather_grads(pieces, g_all, own, count, begin - base, end + 1 - base)
    total[...] = before[...] if chunk else jnp.zeros_like(total)

    def cells_of(sources, part, first, size):
        found = []
        for h in range(loaded):
            low = max(first - base, h * per)
            high = min(first - base + size, (h + 1) * per)
            if low < high:
                found.append(sources[2 * h + part][:, group(low - h * per, high - low)])
        return found[0] if len(found) == 1 else jnp.concatenate(found, axis=1)

    for first, size in steps(begin, end):
        hi, lo = grad_shifts(lambda g: g_all[:, group(g - begin)], first, size, outs, half)
        a_hi, a_lo = [
            jnp.concatenate([cells_of(v, part, first, size) for v in (halos, planes_x)], axis=0) for part in range(2)
        ]
        total[...] += lax.dot_general(
            jnp.concatenate([a_hi, a_hi, a_lo], axis=1),
            jnp.concatenate([hi, lo, hi], axis=1),
            (((1,), (1,)), ((), ())),
            preferred_element_type=F32,
        )
    if not last:
        out[0][...] = total[...]
        return
    kept, sent, packed = out

    def tap_block(tap, side):
        p, q, r = tap // 9, tap // 3 % 3, tap % 3
        (rho, sb), (gamma, sc) = PLACE[q], PLACE[r]
        top = ((p * 2 + rho) * 2 + gamma) * chans
        block = total[top : top + chans, group(sb)]
        return block if sc == side else pltpu.roll(block, outs, 1)

    left_side = lane_of((chans, LANES)) < outs
    for tap in range(14):
        right = tap_block(tap + 14, 1) if tap + 14 < 27 else jnp.zeros((chans, LANES), F32)
        packed[tap * chans : (tap + 1) * chans, :] = jnp.where(left_side, tap_block(tap, 0), right)
    size = 7 * chans
    side = lax.rem(lax.axis_index("space"), 2)
    kept[...] = packed[pl.ds(pl.multiple_of(side * size, size), size), :]
    sent[...] = packed[pl.ds(pl.multiple_of((1 - side) * size, size), size), :]


def back_kernel(dims, own, count, begin, end, low, high, *refs):
    chans, outs, planes, height, half = dims
    loaded = high - low
    here, above = refs[: loaded * count], refs[loaded * count : 2 * loaded * count]
    weights = refs[2 * loaded * count][...]
    out, g_here, g_above, grown, sem = refs[-5:]
    base = low * (height // 4 // CHUNKS)
    gather_grads(here, g_here, own, count, begin - base, end + 1 - base)
    gather_grads(above, g_above, own, count, begin - base, end + 1 - base)
    flat = grown.reshape(chans * planes * height, LANES)
    matrix = pairing(half, True)
    matrix = jnp.concatenate([matrix, matrix], axis=0)
    for first, size in steps(begin, end):
        hi, lo = grad_shifts(lambda g: g_here[:, group(g - begin)], first, size, outs, half)
        hi_above, lo_above = grad_shifts(lambda g: g_above[:, group(g - begin)], first, size, outs, half)
        grad = jnp.dot(
            weights,
            jnp.concatenate([hi, lo, hi, hi_above, lo_above, hi_above], axis=0),
            preferred_element_type=F32,
        )
        tiles = []
        for parity in range(planes * 2):
            for j in range(size):
                tops = [(parity * 2 + column) * chans for column in range(2)]
                tiles.append(jnp.concatenate([grad[t : t + chans, group(j)] for t in tops], axis=1))
        hi, lo = split(jnp.concatenate(tiles, axis=0))
        rows = jnp.dot(jnp.concatenate([hi, lo], axis=1), matrix, preferred_element_type=F32)
        for parity in range(planes * 2):
            for j in range(size):
                start = (parity * size + j) * chans
                row = (parity // 2) * height + 4 * (first + j) + parity % 2
                for side in range(2):
                    flat[pl.ds(row + 2 * side, chans, stride=planes * height), :] = rows[
                        start : start + chans, group(side)
                    ]
    part = pl.ds(4 * begin, 4 * (end - begin))
    copy = pltpu.make_async_copy(grown.at[:, part, :], out.at[:, part, :], sem)
    copy.start()
    copy.wait()


def flat_kernel(half, cube, flat):
    own, cells = flat.shape
    for g in range(cells // LANES):
        sides = [cube[pl.ds(2 * g + side, own, stride=cells // half), :] for side in range(2)]
        flat[:, group(g)] = jnp.concatenate(sides, axis=1)


def activation_kernel(half, h, chunk, *refs):
    out, cube, sem = refs[-3:]
    own, cells = chunk.shape
    rows = cells // half
    for g in range(cells // LANES):
        x = chunk[:, group(g)]
        value = jnp.maximum(x, 0.0) + jnp.log1p(jnp.exp(-jnp.abs(x)))
        cube[pl.ds(2 * g, own, stride=rows), :] = value[:, :half]
        cube[pl.ds(2 * g + 1, own, stride=rows), :] = value[:, half:]
    copies = []
    for i in range(own):
        target = out.at[pl.ds((i * CHUNKS + h) * rows, rows), :]
        copies.append(pltpu.make_async_copy(cube.at[pl.ds(i * rows, rows), :], target, sem.at[i]))
        copies[-1].start()
    for copy in copies:
        copy.wait()


def call(kernel, name, time, shapes, scratch, *args, in_place=False):
    specs = [VMEM] * len(args)
    if in_place:
        specs[-1] = ANY
    return pl.pallas_call(
        kernel,
        name=name,
        out_shape=[jax.ShapeDtypeStruct(s, t) for s, t in shapes],
        in_specs=specs,
        out_specs=[ANY if name in ("back", "activation") else VMEM] * len(shapes),
        scratch_shapes=scratch,
        input_output_aliases={len(args) - 1: 0} if in_place else {},
        cost_estimate=pl.CostEstimate(flops=0, bytes_accessed=int(time * 3.6e2), transcendentals=0),
        compiler_params=pltpu.CompilerParams(vmem_limit_bytes=12 * 1024 * 1024),
    )(*args)


def turned(value, axis, steps):
    count = lax.axis_size(axis)
    return lax.ppermute(value, axis, [(s, (s + steps) % count) for s in range(count)])


def from_behind(value, axis, steps):
    count = lax.axis_size(axis)
    initial, last = (max(0, -steps), min(count, count - steps))
    return lax.ppermute(value, axis, [(source, source + steps) for source in range(initial, last)])


def sum_over(kept, sent, axis, beside):
    count = lax.axis_size(axis)
    assert count > 1 and not count & (count - 1)

    def swapped(value, bit):
        return lax.ppermute(value, axis, [(s, s ^ bit) for s in range(count)])

    value = beside(0, kept + swapped(sent, 1))
    bit = 2
    while bit < count:
        value = beside(bit.bit_length() - 1, value + swapped(value, bit))
        bit *= 2
    other = swapped(value, 1)
    first = lax.rem(lax.axis_index(axis), 2) == 0
    return jnp.where(first, value, other), jnp.where(first, other, value)


def on_device(volume, filters, cotangent):
    real, planes, height, width = volume.shape
    outs = filters.shape[0]
    own = cotangent.shape[0]
    count = lax.axis_size("chan")
    half = width // 2
    cells = (height // 2) * half
    part_cells = cells // CHUNKS
    assert planes == 2 and width == LANES and height % (4 * STEP * CHUNKS) == 0 and 2 * outs == LANES
    chans = -(-real // 16) * 16
    taps = filters.transpose(2, 3, 4, 1, 0)
    if chans > real:
        volume = jnp.pad(volume, ((0, chans - real), (0, 0), (0, 0), (0, 0)))
        taps = jnp.pad(taps, ((0, 0), (0, 0), (0, 0), (0, chans - real), (0, 0)))
    dims = (chans, outs, planes, height, half)
    rows = height // CHUNKS
    halos = [from_behind(volume[:, -1, h * rows : (h + 1) * rows], "space", 1) for h in range(CHUNKS)]
    halos = [halo.reshape(chans * rows, width) for halo in halos]
    x_own, parts, before = [], [], []
    for h in range(CHUNKS):
        shapes = [((8 * chans, part_cells), BF16)] * 2 + [((outs, part_cells), F32)]
        carry = [((outs, LANES), F32)] if h < CHUNKS - 1 else []
        if h:
            results = call(
                functools.partial(own_kernel, dims, h), "own", 1.6, shapes + carry, [], volume.reshape(-1, width), w_own, *before
            )
            before = results[3:]
        else:
            results = call(
                functools.partial(own_kernel, dims, h),
                "own",
                2.2,
                shapes
                + [
                    ((4 * outs, 24 * chans), BF16),
                    ((4 * outs, 12 * chans), BF16),
                    ((8 * chans, 24 * outs), BF16),
                    ((outs, LANES), F32),
                ],
                [pltpu.VMEM((12 * chans, 4 * outs), F32)],
                volume.reshape(-1, width),
                taps.reshape(27 * chans, outs),
            )
            w_own, w_halo, w_back, carried = results[3:]
            before = [carried]
        x_own += results[:2]
        parts.append(results[2])
    (upstream,) = call(
        functools.partial(flat_kernel, half), "flat", 0.8, [((own, cells), F32)], [], cotangent.reshape(-1, half)
    )
    x_halos, grads, above, carry, activated = [], [], [], [], []

    def activate(h, preact, *before):
        return call(
            functools.partial(activation_kernel, half, h),
            "activation",
            1.0,
            [((own * (height // 2), half), F32)],
            [pltpu.VMEM((own * (height // 2 // CHUNKS), half), F32), pltpu.SemaphoreType.DMA((own,))],
            preact,
            *before,
            in_place=bool(h),
        )

    for h in range(CHUNKS):
        shapes = [((4 * chans, part_cells), BF16)] * 2 + [((own, part_cells), F32)] * count
        if h < CHUNKS - 1:
            shapes.append(((outs, LANES), F32))
        xh_hi, xh_lo, *pieces = call(
            functools.partial(halo_kernel, dims, own, count, h),
            "halo",
            1.7,
            shapes,
            [pltpu.VMEM((outs, part_cells), F32)],
            halos[h],
            parts[h],
            w_halo,
            *carry,
        )
        x_halos += [xh_hi, xh_lo]
        carry = pieces[count:]
        preact = pieces[0]
        if h:
            preact, activated = lax.optimization_barrier((preact, activated))
        for k in range(1, count):
            preact = preact + turned(pieces[k], "chan", k)
        grad = upstream[:, h * part_cells : (h + 1) * part_cells] * jax.nn.sigmoid(preact)
        above.append([from_behind(grad, "space", -1)])
        grads.append([grad] + [turned(grad, "chan", k) for k in range(1, count)])
        if h < CHUNKS - 1:
            activated = list(activate(h, preact, *activated))
    for h in range(CHUNKS - 1):
        sent = grads[h][1:]
        above[h] += [from_behind(g, "space", -1) for g in sent]

    summed = []
    for h in range(CHUNKS):
        low = max(h - 1, 0)
        last = h == CHUNKS - 1
        sources = sum(grads[low : h + 1], [])
        if not last:
            sources[0], above[h][0] = lax.optimization_barrier((sources[0], above[h][0]))
        if last:
            *early, summed[0] = lax.optimization_barrier((*[chunk[0] for chunk in above], summed[0]))
            for chunk, grad in zip(above, early):
                chunk[0] = grad
            shown, summed[0] = lax.optimization_barrier((preact, summed[0]))
            activated = list(activate(CHUNKS - 1, shown, *activated))
            *sent, summed[0], activated[0] = lax.optimization_barrier((*grads[-1][1:], summed[0], activated[0]))
            above[-1] += [from_behind(g, "space", -1) for g in sent]
        summed = call(
            functools.partial(filter_kernel, dims, own, count, h),
            "filter",
            1.6,
            [((7 * chans, LANES), F32)] * 2 if last else [((12 * chans, 4 * outs), F32)],
            ([pltpu.VMEM((14 * chans, LANES), F32)] if last else [])
            + [
                pltpu.VMEM((12 * chans, 4 * outs), F32),
                pltpu.VMEM((outs, part_cells + (LANES * (2 if last else 1) if h else 0)), F32),
            ],
            *sources,
            *x_own[2 * low : 2 * h + 2],
            *x_halos[2 * low : 2 * h + 2],
            *summed,
        )
        summed = list(summed)
    per = height // 4 // CHUNKS
    cuts = [0] + [height // 4 * share // 32 // 2 * 2 for share in BACK] + [height // 4]
    state = {"grad": [], "done": 0}

    def rows_of_grad(value):
        i = state["done"]
        begin, end = cuts[i], cuts[i + 1]
        low, high = begin // per, min(end // per + 1, CHUNKS)
        sources = sum(grads[low:high], []) + sum(above[low:high], [])
        *sources, value = lax.optimization_barrier((*sources, value))
        state["grad"] = call(
            functools.partial(back_kernel, dims, own, count, begin, end, low, high),
            "back",
            2.5,
            [((chans * planes, height, width), F32)],
            [pltpu.VMEM((outs, (end + 1 - begin) * LANES), F32)] * 2
            + [pltpu.VMEM((chans * planes, height, width), F32), pltpu.SemaphoreType.DMA],
            *sources,
            w_back,
            *state["grad"],
            in_place=bool(i),
        )
        state["done"] += 1
        return value

    def beside(index, value):
        if state["grad"]:
            *state["grad"], value = lax.optimization_barrier((*state["grad"], value))
        return rows_of_grad(value) if state["done"] < len(cuts) - 1 else value

    low, high = sum_over(*summed, "space", beside)
    while state["done"] < len(cuts) - 1:
        low = rows_of_grad(low)
    (volume_grad,) = state["grad"]
    (activated,) = activated
    volume_grad = volume_grad.reshape(chans, planes, height, width)[:real]
    depth_all = planes * lax.axis_size("space")
    factor = float(depth_all // 2 * (height // 2) * half) ** (-0.5)
    unpacked = jnp.concatenate([low[:, :outs], high[:, :outs], low[:, outs:], high[:-chans, outs:]], axis=0) * factor
    filter_grad = unpacked.reshape(3, 3, 3, chans, outs)[:, :, :, :real].transpose(4, 3, 0, 1, 2)
    return (activated.reshape(cotangent.shape), volume_grad, filter_grad)


def solution(mesh):
    in_specs = (
        P("chan", "space", None, None),
        P(None, "chan", None, None, None),
        P("chan", "space", None, None),
    )
    out_specs = (
        P("chan", "space", None, None),
        P("chan", "space", None, None),
        P(None, "chan", None, None, None),
    )
    return jax.shard_map(
        on_device, mesh=mesh, in_specs=in_specs, out_specs=out_specs, check_vma=False
    )
```

```python
import functools

import jax
import jax.numpy as jnp
from jax import lax
from jax.experimental import pallas as pl
from jax.experimental.pallas import tpu as pltpu
from jax.sharding import PartitionSpec as P

F32 = jnp.float32
BF16 = jnp.bfloat16
LANES = 128
STEP = 8
CHUNKS = 2
BACK = (10, 22)
VMEM = pl.BlockSpec(memory_space=pltpu.VMEM)
ANY = pl.BlockSpec(memory_space=pl.ANY)

PLACE = {0: (1, 1), 1: (0, 0), 2: (1, 0)}


def split(x):
    hi = x.astype(BF16)
    return hi, (x - hi.astype(F32)).astype(BF16)


def pairing(half, transposed):
    size = 4 * half
    cell = lax.broadcasted_iota(jnp.int32, (size, size), 0 if transposed else 1)
    source = lax.broadcasted_iota(jnp.int32, (size, size), 1 if transposed else 0)
    parity, rest = cell // (2 * half), cell % (2 * half)
    wanted = (rest // half) * (2 * half) + 2 * (rest % half) + parity
    return (source == wanted).astype(F32).astype(BF16)


def steps(begin, end):
    runs = -(-(end - begin) // (STEP + 1))
    cuts = [begin + (end - begin) * i // runs for i in range(runs + 1)]
    return [(low, high - low) for low, high in zip(cuts, cuts[1:])]


def lane_of(shape):
    return lax.broadcasted_iota(jnp.int32, shape, 1)


def group(index, count=1):
    return slice(index * LANES, (index + count) * LANES)


def parity_split(load, planes, first, matrix):
    tiles = []
    for plane in range(planes):
        for parity in range(2):
            for j in range(STEP):
                row = 4 * (first + j) + parity
                tiles.append(jnp.concatenate([load(plane, row), load(plane, row + 2)], axis=1))
    chans = tiles[0].shape[0]
    hi, lo = split(jnp.concatenate(tiles, axis=0))
    moved = jnp.dot(jnp.concatenate([hi, lo], axis=0), matrix, preferred_element_type=F32).astype(BF16)
    parts = []
    for part in range(2):
        rows = []
        for parity in range(planes * 2):
            for column in range(2):
                pieces = []
                for j in range(STEP):
                    start = ((part * planes * 2 + parity) * STEP + j) * chans
                    pieces.append(moved[start : start + chans, group(column)])
                rows.append(jnp.concatenate(pieces, axis=1))
        parts.append(jnp.concatenate(rows, axis=0))
    return parts


def shift_add(y, outs, half, carry):
    lane = lane_of((outs, LANES))
    first_column = lane % half == 0
    first_row = lane < half

    def one_column(v):
        return jnp.where(first_column, 0.0, pltpu.roll(v, 1, 1))

    pieces = []
    for j in range(STEP):
        v = [y[s * outs : (s + 1) * outs, group(j)] for s in range(4)]
        here = v[0] + one_column(v[1])
        late = pltpu.roll(v[2] + one_column(v[3]), half, 1)
        pieces.append(here + jnp.where(first_row, carry, late))
        carry = late
    return jnp.concatenate(pieces, axis=1), carry


def grad_shifts(load, first, count, outs, half):
    lane = lane_of((outs, LANES))
    last_column = lane % half == half - 1
    first_row = lane < half

    def one_column(v):
        return jnp.where(last_column, 0.0, pltpu.roll(v, LANES - 1, 1))

    v = [load(first + j) for j in range(count + 1)]
    swapped = [pltpu.roll(a, half, 1) for a in v]
    pieces = []
    for j in range(count):
        later = jnp.where(first_row, swapped[j], swapped[j + 1])
        pieces.append(jnp.concatenate([v[j], one_column(v[j]), later, one_column(later)], axis=0))
    return split(jnp.concatenate(pieces, axis=1))


def gather_grads(pieces, scratch, own, count, begin, end):
    me = lax.axis_index("chan")
    per = pieces[0].shape[1] // LANES
    chunks = len(pieces) // count
    for chunk in range(chunks):
        low, high = max(begin, chunk * per), min(end, (chunk + 1) * per)
        for k in range(count):
            start = pl.multiple_of(lax.rem(me + count - k, count) * own, own)
            piece = pieces[chunk * count + k]
            scratch[pl.ds(start, own), group(low - begin, high - low)] = piece[:, group(low - chunk * per, high - low)]
    if end > chunks * per:
        scratch[:, group(chunks * per - begin)] = jnp.zeros((scratch.shape[0], LANES), F32)


def own_kernel(dims, chunk, vol, *refs):
    chans, outs, planes, height, half = dims
    rows = height // CHUNKS
    if chunk:
        w_own, before = refs[:2]
        x_hi, x_lo, part, *rest = refs[2:]
        carry, weights = before[...], w_own[...]
        after = rest[0] if rest else None
    else:
        filt, x_hi, x_lo, part, w_own, w_halo, w_back, after, w_t = refs
        carry, weights = jnp.zeros((outs, LANES), F32), lay_weights(dims, filt, w_t, w_own, w_halo, w_back)
    matrix = pairing(half, False)

    def load(plane, row):
        return vol[pl.ds(plane * height + chunk * rows + row, chans, stride=planes * height), :]

    for first in range(0, rows // 4, STEP):
        hi, lo = parity_split(load, planes, first, matrix)
        cells = group(first, STEP)
        x_hi[:, cells] = hi
        x_lo[:, cells] = lo
        y = jnp.dot(weights, jnp.concatenate([hi, lo, hi], axis=0), preferred_element_type=F32)
        part[:, cells], carry = shift_add(y, outs, half, carry)
    if after is not None:
        after[...] = carry


def lay_weights(dims, filt, w_t, w_own, w_halo, w_back):
    chans, outs, planes, height, half = dims
    w_t[...] = jnp.zeros_like(w_t)
    for p in range(3):
        for q in range(3):
            for r in range(3):
                (rho, sb), (gamma, sc) = PLACE[q], PLACE[r]
                top = ((p * 2 + rho) * 2 + gamma) * chans
                left = (sb * 2 + sc) * outs
                tap = (p * 3 + q) * 3 + r
                w_t[top : top + chans, left : left + outs] = filt[tap * chans : (tap + 1) * chans, :]
    edge = 4 * chans
    hi, lo = split(w_t[...])
    here = jnp.concatenate([hi[edge:], hi[edge:], lo[edge:]], axis=1)
    above = jnp.concatenate([hi[:edge], hi[:edge], lo[:edge]], axis=1)
    w_back[...] = jnp.concatenate([here, jnp.concatenate([jnp.zeros_like(above), above], axis=0)], axis=1)
    hi, lo = hi.astype(F32), lo.astype(F32)
    w_halo[...] = jnp.concatenate([hi[:edge], hi[:edge], lo[:edge]], axis=0).T.astype(BF16)
    hi, lo = split(w_t[edge:, :].T)
    weights = jnp.concatenate([hi, hi, lo], axis=1)
    w_own[...] = weights
    return weights


def halo_kernel(dims, own, count, chunk, *refs):
    chans, outs, planes, height, half = dims
    plane, part, w_halo = refs[:3]
    before = refs[3] if chunk else None
    x_hi, x_lo, *results, total = refs[4 if chunk else 3 :]
    after = results[count] if len(results) > count else None
    matrix = pairing(half, False)
    weights = w_halo[...]
    rows = height // CHUNKS

    def load(_, row):
        return plane[pl.ds(row, chans, stride=rows), :]

    carry = before[...] if chunk else jnp.zeros((outs, LANES), F32)
    for first in range(0, rows // 4, STEP):
        hi, lo = parity_split(load, 1, first, matrix)
        cells = group(first, STEP)
        x_hi[:, cells] = hi
        x_lo[:, cells] = lo
        y = jnp.dot(weights, jnp.concatenate([hi, lo, hi], axis=0), preferred_element_type=F32)
        added, carry = shift_add(y, outs, half, carry)
        total[:, cells] = part[:, cells] + added
    if after is not None:
        after[...] = carry
    me = lax.axis_index("chan")
    for k in range(count):
        start = pl.multiple_of(lax.rem(me + k, count) * own, own)
        results[k][...] = total[pl.ds(start, own), :]


def filter_kernel(dims, own, count, chunk, *refs):
    chans, outs, planes, height, half = dims
    per = height // 4 // CHUNKS
    loaded = min(chunk, 1) + 1
    last = chunk == CHUNKS - 1
    pieces, refs = refs[: loaded * count], refs[loaded * count :]
    planes_x, refs = refs[: 2 * loaded], refs[2 * loaded :]
    halos, refs = refs[: 2 * loaded], refs[2 * loaded :]
    if chunk:
        before, refs = refs[0], refs[1:]
    *out, total, g_all = refs
    base = (chunk - loaded + 1) * per
    begin = chunk * per - (1 if chunk else 0)
    end = (chunk + 1) * per - (0 if last else 1)
    gather_grads(pieces, g_all, own, count, begin - base, end + 1 - base)
    total[...] = before[...] if chunk else jnp.zeros_like(total)

    def cells_of(sources, part, first, size):
        found = []
        for h in range(loaded):
            low = max(first - base, h * per)
            high = min(first - base + size, (h + 1) * per)
            if low < high:
                found.append(sources[2 * h + part][:, group(low - h * per, high - low)])
        return found[0] if len(found) == 1 else jnp.concatenate(found, axis=1)

    for first, size in steps(begin, end):
        hi, lo = grad_shifts(lambda g: g_all[:, group(g - begin)], first, size, outs, half)
        a_hi, a_lo = [
            jnp.concatenate([cells_of(v, part, first, size) for v in (halos, planes_x)], axis=0) for part in range(2)
        ]
        total[...] += lax.dot_general(
            jnp.concatenate([a_hi, a_hi, a_lo], axis=1),
            jnp.concatenate([hi, lo, hi], axis=1),
            (((1,), (1,)), ((), ())),
            preferred_element_type=F32,
        )
    if not last:
        out[0][...] = total[...]
        return
    kept, sent, packed = out

    def tap_block(tap, side):
        p, q, r = tap // 9, tap // 3 % 3, tap % 3
        (rho, sb), (gamma, sc) = PLACE[q], PLACE[r]
        top = ((p * 2 + rho) * 2 + gamma) * chans
        block = total[top : top + chans, group(sb)]
        return block if sc == side else pltpu.roll(block, outs, 1)

    left_side = lane_of((chans, LANES)) < outs
    for tap in range(14):
        right = tap_block(tap + 14, 1) if tap + 14 < 27 else jnp.zeros((chans, LANES), F32)
        packed[tap * chans : (tap + 1) * chans, :] = jnp.where(left_side, tap_block(tap, 0), right)
    size = 7 * chans
    side = lax.rem(lax.axis_index("space"), 2)
    kept[...] = packed[pl.ds(pl.multiple_of(side * size, size), size), :]
    sent[...] = packed[pl.ds(pl.multiple_of((1 - side) * size, size), size), :]


def back_kernel(dims, own, count, begin, end, low, high, *refs):
    chans, outs, planes, height, half = dims
    loaded = high - low
    here, above = refs[: loaded * count], refs[loaded * count : 2 * loaded * count]
    weights = refs[2 * loaded * count][...]
    out, g_here, g_above, grown, sem = refs[-5:]
    base = low * (height // 4 // CHUNKS)
    gather_grads(here, g_here, own, count, begin - base, end + 1 - base)
    gather_grads(above, g_above, own, count, begin - base, end + 1 - base)
    flat = grown.reshape(chans * planes * height, LANES)
    matrix = pairing(half, True)
    matrix = jnp.concatenate([matrix, matrix], axis=0)
    for first, size in steps(begin, end):
        hi, lo = grad_shifts(lambda g: g_here[:, group(g - begin)], first, size, outs, half)
        hi_above, lo_above = grad_shifts(lambda g: g_above[:, group(g - begin)], first, size, outs, half)
        grad = jnp.dot(
            weights,
            jnp.concatenate([hi, lo, hi, hi_above, lo_above, hi_above], axis=0),
            preferred_element_type=F32,
        )
        tiles = []
        for parity in range(planes * 2):
            for j in range(size):
                tops = [(parity * 2 + column) * chans for column in range(2)]
                tiles.append(jnp.concatenate([grad[t : t + chans, group(j)] for t in tops], axis=1))
        hi, lo = split(jnp.concatenate(tiles, axis=0))
        rows = jnp.dot(jnp.concatenate([hi, lo], axis=1), matrix, preferred_element_type=F32)
        for parity in range(planes * 2):
            for j in range(size):
                start = (parity * size + j) * chans
                row = (parity // 2) * height + 4 * (first + j) + parity % 2
                for side in range(2):
                    flat[pl.ds(row + 2 * side, chans, stride=planes * height), :] = rows[
                        start : start + chans, group(side)
                    ]
    part = pl.ds(4 * begin, 4 * (end - begin))
    copy = pltpu.make_async_copy(grown.at[:, part, :], out.at[:, part, :], sem)
    copy.start()
    copy.wait()


def flat_kernel(half, cube, flat):
    own, cells = flat.shape
    for g in range(cells // LANES):
        sides = [cube[pl.ds(2 * g + side, own, stride=cells // half), :] for side in range(2)]
        flat[:, group(g)] = jnp.concatenate(sides, axis=1)


def activation_kernel(half, h, chunk, *refs):
    out, cube, sem = refs[-3:]
    own, cells = chunk.shape
    rows = cells // half
    for g in range(cells // LANES):
        x = chunk[:, group(g)]
        value = jnp.maximum(x, 0.0) + jnp.log1p(jnp.exp(-jnp.abs(x)))
        cube[pl.ds(2 * g, own, stride=rows), :] = value[:, :half]
        cube[pl.ds(2 * g + 1, own, stride=rows), :] = value[:, half:]
    copies = []
    for i in range(own):
        target = out.at[pl.ds((i * CHUNKS + h) * rows, rows), :]
        copies.append(pltpu.make_async_copy(cube.at[pl.ds(i * rows, rows), :], target, sem.at[i]))
        copies[-1].start()
    for copy in copies:
        copy.wait()


def call(kernel, name, time, shapes, scratch, *args, in_place=False):
    specs = [VMEM] * len(args)
    if in_place:
        specs[-1] = ANY
    return pl.pallas_call(
        kernel,
        name=name,
        out_shape=[jax.ShapeDtypeStruct(s, t) for s, t in shapes],
        in_specs=specs,
        out_specs=[ANY if name in ("back", "activation") else VMEM] * len(shapes),
        scratch_shapes=scratch,
        input_output_aliases={len(args) - 1: 0} if in_place else {},
        cost_estimate=pl.CostEstimate(flops=0, bytes_accessed=int(time * 3.6e2), transcendentals=0),
        compiler_params=pltpu.CompilerParams(vmem_limit_bytes=12 * 1024 * 1024),
    )(*args)


def turned(value, axis, steps):
    count = lax.axis_size(axis)
    return lax.ppermute(value, axis, [(s, (s + steps) % count) for s in range(count)])


def from_behind(value, axis, steps):
    count = lax.axis_size(axis)
    initial, last = (max(0, -steps), min(count, count - steps))
    return lax.ppermute(value, axis, [(source, source + steps) for source in range(initial, last)])


def sum_over(kept, sent, axis, beside):
    count = lax.axis_size(axis)
    assert count > 1 and not count & (count - 1)

    def swapped(value, bit):
        return lax.ppermute(value, axis, [(s, s ^ bit) for s in range(count)])

    value = beside(0, kept + swapped(sent, 1))
    bit = 2
    while bit < count:
        value = beside(bit.bit_length() - 1, value + swapped(value, bit))
        bit *= 2
    other = swapped(value, 1)
    first = lax.rem(lax.axis_index(axis), 2) == 0
    return jnp.where(first, value, other), jnp.where(first, other, value)


def on_device(volume, filters, cotangent):
    real, planes, height, width = volume.shape
    outs = filters.shape[0]
    own = cotangent.shape[0]
    count = lax.axis_size("chan")
    half = width // 2
    cells = (height // 2) * half
    part_cells = cells // CHUNKS
    assert planes == 2 and width == LANES and height % (4 * STEP * CHUNKS) == 0 and 2 * outs == LANES
    chans = -(-real // 16) * 16
    taps = filters.transpose(2, 3, 4, 1, 0)
    if chans > real:
        volume = jnp.pad(volume, ((0, chans - real), (0, 0), (0, 0), (0, 0)))
        taps = jnp.pad(taps, ((0, 0), (0, 0), (0, 0), (0, chans - real), (0, 0)))
    dims = (chans, outs, planes, height, half)
    rows = height // CHUNKS
    ends, source = [volume[:, -1, :rows]], volume
    for h in range(1, CHUNKS):
        source, _ = lax.optimization_barrier((source, ends[-1]))
        ends.append(source[:, -1, h * rows : (h + 1) * rows])
    halos = [from_behind(end, "space", 1) for end in ends]
    halos = [halo.reshape(chans * rows, width) for halo in halos]
    x_own, parts, before = [], [], []
    for h in range(CHUNKS):
        shapes = [((8 * chans, part_cells), BF16)] * 2 + [((outs, part_cells), F32)]
        carry = [((outs, LANES), F32)] if h < CHUNKS - 1 else []
        if h:
            results = call(
                functools.partial(own_kernel, dims, h), "own", 1.6, shapes + carry, [], volume.reshape(-1, width), w_own, *before
            )
            before = results[3:]
        else:
            results = call(
                functools.partial(own_kernel, dims, h),
                "own",
                2.2,
                shapes
                + [
                    ((4 * outs, 24 * chans), BF16),
                    ((4 * outs, 12 * chans), BF16),
                    ((8 * chans, 24 * outs), BF16),
                    ((outs, LANES), F32),
                ],
                [pltpu.VMEM((12 * chans, 4 * outs), F32)],
                volume.reshape(-1, width),
                taps.reshape(27 * chans, outs),
            )
            w_own, w_halo, w_back, carried = results[3:]
            before = [carried]
        x_own += results[:2]
        parts.append(results[2])
    (upstream,) = call(
        functools.partial(flat_kernel, half), "flat", 0.8, [((own, cells), F32)], [], cotangent.reshape(-1, half)
    )
    x_halos, grads, above, carry, activated = [], [], [], [], []

    def activate(h, preact, *before):
        return call(
            functools.partial(activation_kernel, half, h),
            "activation",
            1.0,
            [((own * (height // 2), half), F32)],
            [pltpu.VMEM((own * (height // 2 // CHUNKS), half), F32), pltpu.SemaphoreType.DMA((own,))],
            preact,
            *before,
            in_place=bool(h),
        )

    for h in range(CHUNKS):
        shapes = [((4 * chans, part_cells), BF16)] * 2 + [((own, part_cells), F32)] * count
        if h < CHUNKS - 1:
            shapes.append(((outs, LANES), F32))
        xh_hi, xh_lo, *pieces = call(
            functools.partial(halo_kernel, dims, own, count, h),
            "halo",
            1.7,
            shapes,
            [pltpu.VMEM((outs, part_cells), F32)],
            halos[h],
            parts[h],
            w_halo,
            *carry,
        )
        x_halos += [xh_hi, xh_lo]
        carry = pieces[count:]
        preact = pieces[0]
        if h:
            preact, activated = lax.optimization_barrier((preact, activated))
        for k in range(1, count):
            preact = preact + turned(pieces[k], "chan", k)
        grad = upstream[:, h * part_cells : (h + 1) * part_cells] * jax.nn.sigmoid(preact)
        above.append([from_behind(grad, "space", -1)])
        grads.append([grad] + [turned(grad, "chan", k) for k in range(1, count)])
        if h < CHUNKS - 1:
            activated = list(activate(h, preact, *activated))
    for h in range(CHUNKS - 1):
        sent = grads[h][1:]
        above[h] += [from_behind(g, "space", -1) for g in sent]

    summed = []
    for h in range(CHUNKS):
        low = max(h - 1, 0)
        last = h == CHUNKS - 1
        sources = sum(grads[low : h + 1], [])
        if not last:
            sources[0], above[h][0] = lax.optimization_barrier((sources[0], above[h][0]))
        if last:
            *early, summed[0] = lax.optimization_barrier((*[chunk[0] for chunk in above], summed[0]))
            for chunk, grad in zip(above, early):
                chunk[0] = grad
            shown, summed[0] = lax.optimization_barrier((preact, summed[0]))
            activated = list(activate(CHUNKS - 1, shown, *activated))
            *sent, summed[0], activated[0] = lax.optimization_barrier((*grads[-1][1:], summed[0], activated[0]))
            above[-1] += [from_behind(g, "space", -1) for g in sent]
        summed = call(
            functools.partial(filter_kernel, dims, own, count, h),
            "filter",
            1.6,
            [((7 * chans, LANES), F32)] * 2 if last else [((12 * chans, 4 * outs), F32)],
            ([pltpu.VMEM((14 * chans, LANES), F32)] if last else [])
            + [
                pltpu.VMEM((12 * chans, 4 * outs), F32),
                pltpu.VMEM((outs, part_cells + (LANES * (2 if last else 1) if h else 0)), F32),
            ],
            *sources,
            *x_own[2 * low : 2 * h + 2],
            *x_halos[2 * low : 2 * h + 2],
            *summed,
        )
        summed = list(summed)
    per = height // 4 // CHUNKS
    cuts = [0] + [height // 4 * share // 32 // 2 * 2 for share in BACK] + [height // 4]
    state = {"grad": [], "done": 0}

    def rows_of_grad(value):
        i = state["done"]
        begin, end = cuts[i], cuts[i + 1]
        low, high = begin // per, min(end // per + 1, CHUNKS)
        sources = sum(grads[low:high], []) + sum(above[low:high], [])
        *sources, value = lax.optimization_barrier((*sources, value))
        state["grad"] = call(
            functools.partial(back_kernel, dims, own, count, begin, end, low, high),
            "back",
            2.5,
            [((chans * planes, height, width), F32)],
            [pltpu.VMEM((outs, (end + 1 - begin) * LANES), F32)] * 2
            + [pltpu.VMEM((chans * planes, height, width), F32), pltpu.SemaphoreType.DMA],
            *sources,
            w_back,
            *state["grad"],
            in_place=bool(i),
        )
        state["done"] += 1
        return value

    def beside(index, value):
        if state["grad"]:
            *state["grad"], value = lax.optimization_barrier((*state["grad"], value))
        return rows_of_grad(value) if state["done"] < len(cuts) - 1 else value

    low, high = sum_over(*summed, "space", beside)
    while state["done"] < len(cuts) - 1:
        low = rows_of_grad(low)
    (volume_grad,) = state["grad"]
    (activated,) = activated
    volume_grad = volume_grad.reshape(chans, planes, height, width)[:real]
    depth_all = planes * lax.axis_size("space")
    factor = float(depth_all // 2 * (height // 2) * half) ** (-0.5)
    unpacked = jnp.concatenate([low[:, :outs], high[:, :outs], low[:, outs:], high[:-chans, outs:]], axis=0) * factor
    filter_grad = unpacked.reshape(3, 3, 3, chans, outs)[:, :, :, :real].transpose(4, 3, 0, 1, 2)
    return (activated.reshape(cotangent.shape), volume_grad, filter_grad)


def solution(mesh):
    in_specs = (
        P("chan", "space", None, None),
        P(None, "chan", None, None, None),
        P("chan", "space", None, None),
    )
    out_specs = (
        P("chan", "space", None, None),
        P("chan", "space", None, None),
        P(None, "chan", None, None, None),
    )
    return jax.shard_map(
        on_device, mesh=mesh, in_specs=in_specs, out_specs=out_specs, check_vma=False
    )
```
